32 devices in a mesh: groups: 2 (over y), ctx: 4 (over z), hst: 2 (over x), head: 2 (over core).
Axes of the slice: x: 2, y: 2, z: 4, core: 2. Of those that a mesh axis runs over, the one named last changes fastest.
Arguments:
- hidden: bfloat16 [512, 8, 4096], P(('groups', 'ctx', 'hst', 'head')), parts along dimension 0, may hold values from -6 to 6
- block_owner: int32 [512, 1], P('groups'), parts along dimension 0, may hold values from 0 to 3; in each aligned block of 16 rows (0 to 15, 16 to 31, ...) at most 8 rows name the same one
- norm_gain: float32 [4096], replicated, may hold values from 0.25 to 1.75
- kv_weight: bfloat16 [4096, 1024], P(None, 'hst'), may hold values from -0.09375 to 0.09375
- key_gain: float32 [128], replicated, may hold values from 0.1 to 1.9
- queries: bfloat16 [512, 8192], P(('groups', 'ctx'), ('hst', 'head')), parts along dimension 0, may hold values from -320 to 320
- query_pos: int32 [512], P(('groups', 'ctx')), parts along dimension 0, may hold values from 0 to 2047
Outputs:
- attended: bfloat16 [512, 8192], P(('groups', 'ctx'), ('hst', 'head')), parts along dimension 0
The draws below stay inside these ranges and needn't reach their ends.
There are 2 independent parts, one for each index of `groups`. The reference program is written for one: setup_inputs(seed, part) draws one part's arguments, and reference() takes and returns one part's arrays. A program takes and returns all parts, laid end to end along the dimension named above; an argument that names none is the same for every part. Nothing has to cross between parts.
Inputs may be any that keep to these rules, and one draw needn't show every extreme that they name: Within the 16 rows of block_owner held by one source device, no stop is named more than 8 times; every stop owns some block.
All inputs are finite; a program needn't handle non-finite values.
Results may differ from the reference program's by a relative error of at most 0.0045.
The reference program's roundings to bfloat16 on the way count: a program that leaves them out, or rounds other values in their place, can miss the bound.
Values may be sent and summed in bfloat16 or wider, within the bound.
A program may use at most 128 MiB of HBM per device.

```python
import math
import jax
import jax.numpy as jnp
import numpy as np
from jax import lax

D = 4096
QH = 64
KVH = 4
HD = 128
BL = 8
SRC_DEV = 16
CAP = 8
NBLK = 256
QROWS = 256
N_CTX = 4


def draw_queries(key, part):
    base_key = jax.random.fold_in(jax.random.fold_in(key, 17), 0)
    base = jnp.clip(jax.random.normal(base_key, (QROWS, QH, 1, HD), jnp.float32), -4.0, 4.0) * 2.0
    return base.reshape(QROWS, QH * HD).astype(jnp.bfloat16)


def place_ends(values, own_key, low, high):
    shape = values.shape
    place = [jax.random.randint(jax.random.fold_in(own_key, axis), (), 0, shape[axis]) for axis in range(len(shape))]
    values = values.at[tuple(place)].set(low)
    longest = shape.index(max(shape))
    place[longest] = (place[longest] + 1) % shape[longest]
    return values.at[tuple(place)].set(high)


def block_levels(stream_key, shape, shards, least, largest):
    def one(dim, shards_of):
        draws = jax.random.uniform(jax.random.fold_in(jax.random.fold_in(stream_key, 6), dim), (shards_of,), jnp.float32, least / len(shards), largest / len(shards))
        return jnp.repeat(jnp.exp(draws), shape[dim] // shards_of).reshape((-1,) + (1,) * (len(shape) - dim - 1))

    gain = one(*shards[0])
    for cut in shards[1:]:
        gain = gain * one(*cut)
    return gain


def shared_out(stream_key, own, number, rows, number_of, top, limit, skew):
    ranking = jax.random.permutation(stream_key, number_of)
    crowded, common = shares(number_of, rows * top, limit, skew, True), shares(number_of, rows * top, limit, skew, False)
    places = jnp.arange(number_of)

    def named(sizes, rotation):
        used = int((sizes > 0).sum())
        fixed = max(1, used // 4)
        shifted = fixed + (places - fixed + rotation * (used - fixed)) % max(1, number_of - fixed)
        return jnp.zeros((number_of,), jnp.int32).at[ranking[jnp.where(places < fixed, places, shifted)]].set(jnp.asarray(sizes, jnp.int32))

    sizes = jnp.where(number % 4 == 0, named(crowded, number // 4), named(common, number - number // 4 - 1))
    mixed = jax.random.permutation(jax.random.fold_in(own, 3), number_of)
    source_of, sink = mixed[0:number_of // 2 * 2:2], mixed[1:number_of // 2 * 2:2]
    margin = jnp.minimum(sizes[source_of] - 1, limit - sizes[sink]) // 2
    margin = jnp.where((source_of == ranking[0]) | (sink == ranking[0]) | (sizes[sink] == 0), 0, jnp.maximum(margin, 0))
    shifted = jax.random.randint(jax.random.fold_in(own, 4), (number_of // 2,), 0, 1 << 20) % (margin + 1)
    sizes = sizes.at[source_of].add(-shifted).at[sink].add(shifted)
    labels = jnp.searchsorted(jnp.cumsum(sizes), jnp.arange(rows * top), side="right").astype(jnp.int32)
    grid = labels.reshape(top, rows).T
    grid = grid[jax.random.permutation(jax.random.fold_in(own, 1), rows)]
    rotation = jax.random.randint(jax.random.fold_in(own, 2), (rows, 1), 0, top)
    return jnp.take_along_axis(grid, (jnp.arange(top)[None, :] + rotation) % top, axis=1)


def shares(amount, total, limit, skew, full):
    portions = [(1 << 20) // math.isqrt(grade ** skew) + 1 for grade in range(1, amount + 1)]
    largest = limit if full else min(limit, max(-(-total // amount), total * portions[0] // sum(portions)))
    least = 1 if total - largest >= amount - 1 else 0
    given, spare = [largest] + [least] * (amount - 1), total - largest - least * (amount - 1)
    while spare > 0:
        movable = [i for i in range(1, amount) if given[i] < largest] or [i for i in range(1, amount) if given[i] < limit]
        mass, left = sum([portions[i] for i in movable]), spare
        for i in movable:
            more = min(limit - given[i], max(1, left * portions[i] // mass), spare)
            given[i] = given[i] + more
            spare = spare - more
    return np.array(given)


def scatter_about(own_key, dims, scale, most, cuts=(), held_as=jnp.bfloat16):
    drawn = scale * jax.random.normal(own_key, dims, jnp.float32)
    if cuts:
        drawn = drawn * block_levels(own_key, dims, cuts, -0.22, 0.18)
    return jnp.clip(drawn, -most, most).astype(held_as)


def setup_inputs(seed: int = 0, part: int = 0) -> dict:
    streams_of = jax.random.split(jax.random.key(seed), 8)
    own_keys = jax.random.split(jax.random.fold_in(streams_of[7], part), 8)
    hidden = scatter_about(own_keys[0], (NBLK, BL, D), 1.0, 6.0, ((0, 16),))
    block_owner_keys = jax.random.split(jax.random.fold_in(own_keys[1], 1), NBLK // SRC_DEV)
    block_owner_turns = jax.random.permutation(jax.random.fold_in(own_keys[1], 3), NBLK // SRC_DEV)
    block_owner = jax.vmap(lambda own, number: shared_out(jax.random.fold_in(own_keys[1], 2), own, number, SRC_DEV, N_CTX, 1, CAP, 2))(block_owner_keys, block_owner_turns).reshape((NBLK, 1))
    norm_gain = jnp.clip(1.0 + 0.15 * jax.random.normal(streams_of[2], (D,), jnp.float32), 0.25, 1.75)
    kv_weight = scatter_about(streams_of[3], (D, KVH * 2 * HD), D ** -0.5, 0.09375, ((1, 2),))
    key_gain = jnp.clip(1.0 + 0.18 * jax.random.normal(streams_of[4], (HD,), jnp.float32), 0.1, 1.9)
    queries = draw_queries(jax.random.fold_in(jax.random.fold_in(streams_of[7], part), 71), part)
    query_pos = place_ends(jax.random.randint(own_keys[6], (QROWS,), 0, NBLK * BL), jax.random.fold_in(own_keys[6], 1), 0, (NBLK * BL) - 1).astype(jnp.int32)
    return {"hidden": hidden, "block_owner": block_owner, "norm_gain": norm_gain, "kv_weight": kv_weight, "key_gain": key_gain, "queries": queries, "query_pos": query_pos}


EPS = 1e-06
THETA = 1000000.0

def block_starts(owner, n_stop, rows):
    onehot = (owner[:, None] == jnp.arange(n_stop, dtype=jnp.int32)[None, :]).astype(jnp.int32)
    counts = lax.optimization_barrier(jnp.sum(onehot, axis=0))
    before = jnp.cumsum(counts) - counts
    ranks = lax.optimization_barrier(jnp.sum(jnp.cumsum(onehot, axis=0) * onehot, axis=1)) - 1
    return ((lax.optimization_barrier(jnp.sum(onehot * before[None, :], axis=1)) + ranks) * rows).astype(jnp.int32)

def rotate(values, positions):
    half = values.shape[-1] // 2
    freq = THETA ** (-(jnp.arange(half, dtype=jnp.float32) * 2.0) / values.shape[-1])
    angle = positions.astype(jnp.float32)[:, None, None] * freq[None, None, :]
    cosine = jnp.cos(angle)
    sine = jnp.sin(angle)
    first = values[..., :half]
    second = values[..., half:]
    return jnp.concatenate([first * cosine - second * sine, second * cosine + first * sine], axis=-1)

def reference(hidden, block_owner, norm_gain, kv_weight, key_gain, queries, query_pos):
    owner = block_owner[:, 0]
    starts = block_starts(owner, N_CTX, BL)
    key_pos = (starts[:, None] + jnp.arange(BL, dtype=jnp.int32)[None, :]).reshape(-1)
    rows = hidden.reshape(-1, D).astype(jnp.float32)
    normed = (rows * lax.rsqrt(lax.optimization_barrier(jnp.mean(rows * rows, axis=-1, keepdims=True)) + EPS) * norm_gain).astype(jnp.bfloat16)
    proj = jnp.dot(normed, kv_weight, preferred_element_type=jnp.float32).reshape(-1, KVH, 2, HD)
    raw_keys = proj[:, :, 0]
    raw_keys = raw_keys * lax.rsqrt(lax.optimization_barrier(jnp.mean(raw_keys * raw_keys, axis=-1, keepdims=True)) + EPS) * key_gain
    keys = rotate(raw_keys, key_pos).astype(jnp.bfloat16)
    values = proj[:, :, 1].astype(jnp.bfloat16)
    rotated = rotate(queries.astype(jnp.float32).reshape(QROWS, QH, HD), query_pos).astype(jnp.bfloat16)
    scale = 1.0 / math.sqrt(HD)
    allowed = key_pos[None, :] <= query_pos[:, None]
    group = QH // KVH

    def one_head(head):
        kv_head = head // group
        q_head = lax.dynamic_index_in_dim(rotated, head, 1, keepdims=False)
        k_head = lax.dynamic_index_in_dim(keys, kv_head, 1, keepdims=False)
        v_head = lax.dynamic_index_in_dim(values, kv_head, 1, keepdims=False)
        scores = jnp.dot(q_head, k_head.T, preferred_element_type=jnp.float32) * scale
        kept = jnp.where(allowed, scores, -1e+30)
        top = lax.optimization_barrier(jnp.max(kept, axis=1, keepdims=True))
        weights = jnp.where(allowed, jnp.exp(kept - top), 0.0)
        total = lax.optimization_barrier(jnp.sum(weights, axis=1, keepdims=True))
        mixed = jnp.dot(weights.astype(jnp.bfloat16), v_head, preferred_element_type=jnp.float32)
        return (mixed / total).astype(jnp.bfloat16)
    heads = lax.map(one_head, jnp.arange(QH, dtype=jnp.int32))
    return jnp.transpose(heads, (1, 0, 2)).reshape(QROWS, QH * HD)
```

```python
import functools
import math

import jax
import jax.numpy as jnp
import numpy as np
from jax import lax
from jax.experimental import pallas as pl
from jax.experimental.pallas import tpu as pltpu
from jax.sharding import PartitionSpec as P

EPS = 1e-06
THETA = 1000000.0
CHUNKS = (64, 32, 16, 16)
GROUPS = ((3, 0, 64), (4, 64, 32), (4, 96, 32))
OWN_AFTER = 1
TILE = 8
STEP = 256
VMEM_LIMIT = 40 * 2**20
MESH = pl.DeviceIdType.MESH


def rotate(values, positions):
    half = values.shape[-1] // 2
    freq = THETA ** (-(jnp.arange(half, dtype=jnp.float32) * 2.0) / values.shape[-1])
    angle = positions.astype(jnp.float32)[:, None, None] * freq[None, None, :]
    cosine = jnp.cos(angle)
    sine = jnp.sin(angle)
    first = values[..., :half]
    second = values[..., half:]
    return jnp.concatenate(
        [first * cosine - second * sine, second * cosine + first * sine], axis=-1
    )


def normalize(rows, norm_gain):
    wide = rows.astype(jnp.float32)
    scaled = wide * lax.rsqrt(jnp.mean(wide * wide, axis=-1, keepdims=True) + EPS) * norm_gain
    return scaled.astype(jnp.bfloat16)


def finish(proj, positions, key_gain, kv_heads, head_size):
    shaped = proj.reshape(proj.shape[0], kv_heads, 2, head_size)
    raw_keys = shaped[:, :, 0]
    raw_keys = (
        raw_keys * lax.rsqrt(jnp.mean(raw_keys * raw_keys, axis=-1, keepdims=True) + EPS) * key_gain
    )
    keys = rotate(raw_keys, positions).astype(jnp.bfloat16)
    values = shaped[:, :, 1].astype(jnp.bfloat16)
    return jnp.stack([keys, values], axis=2).reshape(proj.shape[0], kv_heads * 2 * head_size)


def spread(hidden, block_owner, norm_gain, kv_weight, key_gain, queries, query_pos):
    n_ctx = lax.axis_size("ctx")
    n_hst = lax.axis_size("hst")
    n_head = lax.axis_size("head")
    src_dev, rows_blk, width = hidden.shape
    head_size = key_gain.shape[0]
    kv_dev = kv_weight.shape[1] // (2 * head_size)
    kv_all = kv_dev * n_hst
    q_dev = queries.shape[1] // head_size
    group = q_dev * n_hst * n_head // kv_all
    used = max(1, q_dev // group)
    q_rows = queries.shape[0]
    ctx_i = lax.axis_index("ctx")
    hst_i = lax.axis_index("hst")
    core_i = lax.axis_index("head")
    owner = block_owner[:, 0]
    n_blk = owner.shape[0]
    code = owner * n_blk + jnp.arange(n_blk, dtype=jnp.int32)
    starts = jnp.sum((code[None, :] < code[:, None]).astype(jnp.int32), axis=1) * rows_blk
    key_pos = (starts[:, None] + jnp.arange(rows_blk, dtype=jnp.int32)[None, :]).reshape(
        n_ctx, n_hst, n_head, src_dev * rows_blk
    )
    normed = normalize(hidden.reshape(src_dev * rows_blk, width), norm_gain)
    gathered = lax.all_gather(normed, "hst", axis=0, tiled=True)
    proj = jnp.dot(gathered, kv_weight, preferred_element_type=jnp.float32)
    my_pos = lax.dynamic_index_in_dim(
        lax.dynamic_index_in_dim(key_pos, ctx_i, 0, keepdims=False), core_i, 1, keepdims=False
    ).reshape(-1)
    restored = finish(proj, my_pos, key_gain, kv_dev, head_size)
    rows = restored.shape[0]
    by_head = restored.reshape(rows, kv_dev, 2 * head_size)
    parts = [
        lax.dynamic_slice_in_dim(
            by_head, (hst_i * n_head + c) * q_dev // group - hst_i * kv_dev, used, 1
        )
        for c in range(n_head)
    ]
    mine = lax.all_to_all(jnp.stack(parts), "head", split_axis=0, concat_axis=0, tiled=True)
    full = lax.all_gather(mine.reshape(n_head * rows, used * 2 * head_size), "ctx", axis=0, tiled=True)
    full = full.reshape(-1, used, 2, head_size)
    k_pos = jnp.transpose(key_pos, (0, 2, 1, 3)).reshape(-1)
    rotated = rotate(
        queries.astype(jnp.float32).reshape(q_rows, q_dev, head_size), query_pos
    ).astype(jnp.bfloat16)
    rotated = rotated.reshape(q_rows, used, q_dev // used, head_size)
    scores = jnp.einsum(
        "qagd,kad->agqk", rotated, full[:, :, 0], preferred_element_type=jnp.float32
    ) * (1.0 / math.sqrt(head_size))
    allowed = (k_pos[None, :] <= query_pos[:, None])[None, None]
    kept = jnp.where(allowed, scores, -1e30)
    best = jnp.max(kept, axis=-1, keepdims=True)
    weights = jnp.where(allowed, jnp.exp(kept - best), 0.0)
    total = jnp.sum(weights, axis=-1, keepdims=True)
    mixed = jnp.einsum(
        "agqk,kad->agqd", weights.astype(jnp.bfloat16), full[:, :, 1], preferred_element_type=jnp.float32
    )
    result = mixed / total
    return (
        jnp.transpose(result, (2, 0, 1, 3)).reshape(q_rows, q_dev * head_size).astype(jnp.bfloat16)
    )


def log2_of(value):
    return value.bit_length() - 1


def fused(
    dims, hid_ref, own_hbm, gain_hbm, w_ref, kgain_hbm, q_hbm, qpos_hbm, freq_hbm, out_ref,
    own_ref, gain_ref, kgain_ref, q_ref, qpos_ref, freq_ref, w_v, own_rows, peer_rows, kv_send, kv_buf, q_rot, q_turn, qpos_s, kpos_s, cos_s, sin_s,
    best, total, acc, w_sem, own_sem, small_sem, hid_send, hid_recv, send_sem, recv_sem,
):
    n_ctx, n_hst, n_head, src_dev, rows_blk, chunks = dims
    rows, width = own_rows.shape
    head_size = kgain_ref.shape[1]
    half = head_size // 2
    n_blk = own_ref.shape[1]
    n_src = n_ctx * n_head
    n_chunk = len(chunks)
    firsts = [sum(chunks[:j]) for j in range(n_chunk)]
    q_rows = q_ref.shape[0]
    q_dev = q_ref.shape[1] // head_size
    z = lax.axis_index("ctx")
    x = lax.axis_index("hst")
    c = lax.axis_index("head")
    me = z * n_head + c
    peer = 1 - x
    f32 = jnp.float32

    w_copy = pltpu.make_async_copy(w_ref, w_v, w_sem)
    own_copy = pltpu.make_async_copy(hid_ref, own_rows, own_sem)
    own_copy.start()
    w_copy.start()
    groups = [(0, rows)] + [(rows + row0, count) for _, row0, count in GROUPS]
    small = [
        pltpu.make_async_copy(src, dst, small_sem.at[i])
        for i, (src, dst) in enumerate(
            [
                (own_hbm, own_ref),
                (freq_hbm, freq_ref),
                (gain_hbm, gain_ref),
                (kgain_hbm, kgain_ref),
                (qpos_hbm, qpos_ref),
                (q_hbm, q_ref),
            ]
        )
    ]
    for copy in small:
        copy.start()

    targets = []
    for dz in range(1, n_ctx):
        for core in range(n_head):
            targets.append(({"ctx": lax.rem(z + dz, n_ctx), "head": core}, core, dz))
    for dc in range(1, n_head):
        core = lax.rem(c + dc, n_head)
        targets.append(({"head": core}, core, 0))

    barrier = pltpu.get_barrier_semaphore()
    pl.semaphore_signal(barrier, inc=1, device_id={"hst": peer}, device_id_type=MESH)
    for device, _, _ in targets:
        pl.semaphore_signal(barrier, inc=1, device_id=device, device_id_type=MESH)
    pl.semaphore_wait(barrier, len(targets) + 1)

    def hidden_copy(j):
        part = pl.ds(firsts[j], chunks[j])
        return pltpu.make_async_remote_copy(
            src_ref=hid_ref.at[part],
            dst_ref=peer_rows.at[part],
            send_sem=hid_send.at[j],
            recv_sem=hid_recv.at[j],
            device_id={"hst": peer},
            device_id_type=MESH,
        )

    for j in range(n_chunk):
        hidden_copy(j).start()

    lane = lax.broadcasted_iota(jnp.int32, (n_blk, n_blk), 1)
    sub = lax.broadcasted_iota(jnp.int32, (n_blk, n_blk), 0)
    for copy in small[:2]:
        copy.wait()
    code_row = (own_ref[...] * n_blk + lane[0:1]).astype(f32)
    code_col = jnp.sum(jnp.where(sub == lane, code_row, 0.0), axis=1, keepdims=True)
    start_col = jnp.sum(jnp.where(code_row < code_col, float(rows_blk), 0.0), axis=1, keepdims=True)
    start_row = jnp.sum(jnp.where(code_col < code_row, float(rows_blk), 0.0), axis=0, keepdims=True)

    blk_bits = log2_of(rows_blk)
    freq = freq_ref[...]
    for side in range(2):
        source = x if side == 0 else peer
        base = ((z * n_hst + source) * n_head + c) * src_dev
        r = lax.broadcasted_iota(jnp.int32, (rows, n_blk), 0)
        hit = lax.broadcasted_iota(jnp.int32, (rows, n_blk), 1) == base + (r >> blk_bits)
        pos = jnp.sum(jnp.where(hit, start_row, 0.0), axis=1, keepdims=True)
        pos = pos + (r[:, 0:1] & (rows_blk - 1)).astype(f32)
        angle = pos * freq
        low = lax.broadcasted_iota(jnp.int32, angle.shape, 1) < half
        sine = jnp.sin(angle)
        cos_s[side * rows : (side + 1) * rows] = jnp.cos(angle)
        sin_s[side * rows : (side + 1) * rows] = jnp.where(low, -sine, sine)

    def turned(u, cosine, sine):
        return u * cosine + pltpu.roll(u, half, 1) * sine

    def kv_copy(row0, count, sem_row, target, slot, sem_col):
        device, core, _ = target
        return pltpu.make_async_remote_copy(
            src_ref=kv_send.at[core, pl.ds(row0, count)],
            dst_ref=kv_buf.at[slot, pl.ds(row0, count)],
            send_sem=send_sem.at[sem_row, sem_col],
            recv_sem=recv_sem.at[sem_row, sem_col],
            device_id=device,
            device_id_type=MESH,
        )

    def sem_of(target, core):
        return (target[2] - 1) * n_head + core if target[2] else (n_ctx - 1) * n_head

    def restore(hidden_ref, hrow, row0, count, stage):
        wide = hidden_ref[hrow : hrow + count].astype(f32)
        mean = jnp.mean(wide * wide, axis=-1, keepdims=True)
        normed = (wide * lax.rsqrt(mean + EPS) * gain_ref[...]).astype(jnp.bfloat16)
        proj = jnp.dot(normed, w_v[...], preferred_element_type=f32)
        cosine = cos_s[row0 : row0 + count]
        sine = sin_s[row0 : row0 + count]
        kept = None
        for head in range(n_head):
            at = head * 2 * head_size
            raw = proj[:, at : at + head_size]
            scale = lax.rsqrt(jnp.mean(raw * raw, axis=-1, keepdims=True) + EPS)
            keys = turned(raw * scale * kgain_ref[...], cosine, sine).astype(jnp.bfloat16)
            values = proj[:, at + head_size : at + 2 * head_size].astype(jnp.bfloat16)
            both = jnp.concatenate([keys, values], axis=1)
            kv_send[head, row0 : row0 + count] = both
            kept = both if kept is None else jnp.where(c == head, both, kept)
        kv_buf[me, row0 : row0 + count] = kept
        for target in targets:
            kv_copy(row0, count, stage, target, me, sem_of(target, c)).start()

    for copy in small[2:4]:
        copy.wait()
    own_copy.wait()
    w_copy.wait()
    restore(own_rows, 0, 0, rows, 0)

    for row0, count in groups:
        source = x if row0 < rows else peer
        for at in range(0, n_src * count, 128):
            size = min(128, n_src * count - at)
            t = at + lax.broadcasted_iota(jnp.int32, (size, n_blk), 0)
            s = t >> log2_of(count)
            r = (t & (count - 1)) + row0 % rows
            blk = ((s >> log2_of(n_head)) * n_hst + source) * n_head + (s & (n_head - 1))
            blk = blk * src_dev + (r >> blk_bits)
            hit = lax.broadcasted_iota(jnp.int32, (size, n_blk), 1) == blk
            pos = jnp.sum(jnp.where(hit, start_row, 0.0), axis=1, keepdims=True)
            first = n_src * row0 + at
            kpos_s[first : first + size] = pos + (r[:, 0:1] & (rows_blk - 1)).astype(f32)

    for copy in small[4:]:
        copy.wait()
    row = lax.broadcasted_iota(jnp.int32, (q_rows, q_rows), 0)
    column = lax.broadcasted_iota(jnp.int32, (q_rows, q_rows), 1)
    qpos = jnp.where(row == column, qpos_ref[...].astype(f32), 0.0)
    qpos = jnp.sum(qpos, axis=1, keepdims=True)
    q_angle = qpos * freq
    q_sine = jnp.sin(q_angle)
    low = lax.broadcasted_iota(jnp.int32, q_angle.shape, 1) < half
    q_sine = jnp.where(low, -q_sine, q_sine)
    q_cosine = jnp.cos(q_angle)
    for head in range(q_dev):
        u = q_ref[:, head * head_size : (head + 1) * head_size].astype(f32)
        q_rot[head * q_rows : (head + 1) * q_rows] = turned(u, q_cosine, q_sine)
    q_turn[...] = q_rot[...].T.astype(jnp.bfloat16)
    qpos_row = qpos_ref[...].astype(f32)
    qpos_s[...] = jnp.concatenate([qpos_row] * q_dev, axis=1)
    tile = TILE * q_rows
    best[...] = jnp.full_like(best, -1e30)
    total[...] = jnp.zeros_like(total)
    acc[...] = jnp.zeros_like(acc)
    factor = math.log2(math.e) / math.sqrt(head_size)

    def attend(row0, count, at):
        span = n_src * count
        keys = kv_buf[:, row0 : row0 + count, 0:head_size].reshape(span, head_size)
        values = kv_buf[:, row0 : row0 + count, head_size : 2 * head_size].reshape(span, head_size)
        step = min(STEP, span)

        def block(i, carry):
            part = pl.ds(pl.multiple_of(i * tile, tile), tile)
            q_part = q_turn[:, part]
            qpos_part = qpos_s[:, part]
            top, denom, mix = best[:, part], total[:, part], acc[:, part]
            for first in range(0, span, step):
                scores = jnp.dot(keys[first : first + step], q_part, preferred_element_type=f32)
                kpos = kpos_s[at + first : at + first + step]
                kept = jnp.where(kpos <= qpos_part, scores, -2e30)
                new = jnp.maximum(top, jnp.max(kept, axis=0, keepdims=True))
                weights = jnp.exp2((kept - new) * factor)
                fade = jnp.exp2((top - new) * factor)
                top = new
                denom = denom * fade + jnp.sum(weights, axis=0, keepdims=True)
                mix = mix * fade + lax.dot_general(
                    values[first : first + step],
                    weights.astype(jnp.bfloat16),
                    (((0,), (0,)), ((), ())),
                    preferred_element_type=f32,
                )
            best[:, part] = top
            total[:, part] = denom
            acc[:, part] = mix
            return carry

        lax.fori_loop(0, q_dev * q_rows // tile, block, 0)

    def arrive(row0, count, stage):
        for dz in range(1, n_ctx):
            for core in range(n_head):
                target = (targets[0][0], 0, dz)
                slot = lax.rem(z + n_ctx - dz, n_ctx) * n_head + core
                kv_copy(row0, count, stage, target, slot, sem_of(target, core)).wait_recv()
        for dc in range(1, n_head):
            target = (targets[0][0], 0, 0)
            slot = z * n_head + lax.rem(c + n_head - dc, n_head)
            kv_copy(row0, count, stage, target, slot, sem_of(target, 0)).wait_recv()

    spans = [(0, rows)] + [(rows + firsts[j], chunks[j]) for j in range(n_chunk)]
    plan = [(OWN_AFTER, 0, rows)] + [(after, rows + row0, count) for after, row0, count in GROUPS]
    for stage in range(1, n_chunk + 1):
        hidden_copy(stage - 1).wait_recv()
        restore(peer_rows, firsts[stage - 1], *spans[stage], stage)
        for after, row0, count in plan:
            if after == stage:
                for i, (first, size) in enumerate(spans):
                    if row0 <= first < row0 + count:
                        arrive(first, size, i)
                attend(row0, count, n_src * row0)

    result = (acc[...] / total[...]).T
    for head in range(q_dev):
        out_ref[:, head * head_size : (head + 1) * head_size] = result[
            head * q_rows : (head + 1) * q_rows
        ].astype(out_ref.dtype)
    for j in range(n_chunk):
        hidden_copy(j).wait_send()
    for stage, (row0, count) in enumerate(spans):
        for target in targets:
            kv_copy(row0, count, stage, target, me, sem_of(target, c)).wait_send()


def body(hidden, block_owner, norm_gain, kv_weight, key_gain, queries, query_pos):
    n_ctx = lax.axis_size("ctx")
    n_hst = lax.axis_size("hst")
    n_head = lax.axis_size("head")
    src_dev, rows_blk, width = hidden.shape
    head_size = key_gain.shape[0]
    kv_dev = kv_weight.shape[1] // (2 * head_size)
    q_rows = queries.shape[0]
    q_dev = queries.shape[1] // head_size
    if n_hst != 2 or kv_dev != n_head or n_ctx > 4 or src_dev * rows_blk != sum(CHUNKS):
        return spread(hidden, block_owner, norm_gain, kv_weight, key_gain, queries, query_pos)
    rows = src_dev * rows_blk
    n_chunk = len(CHUNKS)
    n_src = n_ctx * n_head
    n_peer = n_src - 1
    half = head_size // 2
    freq = THETA ** (-(np.arange(half, dtype=np.float64) * 2.0) / head_size)
    freq = jnp.asarray(np.concatenate([freq, freq]).astype(np.float32)[None])
    vmem = pl.BlockSpec(memory_space=pltpu.VMEM)
    hbm = pl.BlockSpec(memory_space=pltpu.HBM)
    bf16, f32 = jnp.bfloat16, jnp.float32
    return pl.pallas_call(
        functools.partial(fused, (n_ctx, n_hst, n_head, src_dev, rows_blk, CHUNKS)),
        out_shape=jax.ShapeDtypeStruct(queries.shape, bf16),
        in_specs=[hbm] * 8,
        out_specs=vmem,
        scratch_shapes=[
            pltpu.VMEM((1, block_owner.shape[0]), jnp.int32),
            pltpu.VMEM((1, width), f32),
            pltpu.VMEM((1, head_size), f32),
            pltpu.VMEM(queries.shape, bf16),
            pltpu.VMEM((1, q_rows), jnp.int32),
            pltpu.VMEM((1, head_size), f32),
            pltpu.VMEM(kv_weight.shape, bf16),
            pltpu.VMEM((rows, width), bf16),
            pltpu.VMEM((rows, width), bf16),
            pltpu.VMEM((n_head, 2 * rows, 2 * head_size), bf16),
            pltpu.VMEM((n_src, 2 * rows, 2 * head_size), bf16),
            pltpu.VMEM((q_dev * q_rows, head_size), f32),
            pltpu.VMEM((head_size, q_dev * q_rows), bf16),
            pltpu.VMEM((1, q_dev * q_rows), f32),
            pltpu.VMEM((n_src * 2 * rows, 1), f32),
            pltpu.VMEM((2 * rows, head_size), f32),
            pltpu.VMEM((2 * rows, head_size), f32),
            pltpu.VMEM((1, q_dev * q_rows), f32),
            pltpu.VMEM((1, q_dev * q_rows), f32),
            pltpu.VMEM((head_size, q_dev * q_rows), f32),
            pltpu.SemaphoreType.DMA,
            pltpu.SemaphoreType.DMA,
            pltpu.SemaphoreType.DMA((6,)),
            pltpu.SemaphoreType.DMA((n_chunk,)),
            pltpu.SemaphoreType.DMA((n_chunk,)),
            pltpu.SemaphoreType.DMA((n_chunk + 1, n_peer)),
            pltpu.SemaphoreType.DMA((n_chunk + 1, n_peer)),
        ],
        compiler_params=pltpu.CompilerParams(
            collective_id=0, has_side_effects=True, vmem_limit_bytes=VMEM_LIMIT
        ),
    )(
        *[
            pltpu.with_memory_space_constraint(array, pltpu.HBM)
            for array in (
                hidden.reshape(rows, width),
                block_owner.reshape(1, -1),
                norm_gain[None],
                kv_weight,
                key_gain[None],
                queries,
                query_pos[None],
                freq,
            )
        ]
    )


def solution(mesh):
    in_specs = (
        P(("groups", "ctx", "hst", "head"), None, None),
        P("groups", None),
        P(),
        P(None, "hst"),
        P(),
        P(("groups", "ctx"), ("hst", "head")),
        P(("groups", "ctx")),
    )
    out_specs = P(("groups", "ctx"), ("hst", "head"))
    return jax.shard_map(body, mesh=mesh, in_specs=in_specs, out_specs=out_specs, check_vma=False)
```

```python
import functools
import math

import jax
import jax.numpy as jnp
import numpy as np
from jax import lax
from jax.experimental import pallas as pl
from jax.experimental.pallas import tpu as pltpu
from jax.sharding import PartitionSpec as P

EPS = 1e-06
THETA = 1000000.0
CHUNKS = (64, 32, 16, 16)
SLICES = 4
PLAN = ((1, 0, 128, 8, 512), (4, 128, 64, 8, 512), (4, 192, 48, 8, 384), (4, 240, 16, 16, 128))
VMEM_LIMIT = 40 * 2**20
MESH = pl.DeviceIdType.MESH


def rotate(values, positions):
    half = values.shape[-1] // 2
    freq = THETA ** (-(jnp.arange(half, dtype=jnp.float32) * 2.0) / values.shape[-1])
    angle = positions.astype(jnp.float32)[:, None, None] * freq[None, None, :]
    cosine = jnp.cos(angle)
    sine = jnp.sin(angle)
    first = values[..., :half]
    second = values[..., half:]
    return jnp.concatenate(
        [first * cosine - second * sine, second * cosine + first * sine], axis=-1
    )


def normalize(rows, norm_gain):
    wide = rows.astype(jnp.float32)
    scaled = wide * lax.rsqrt(jnp.mean(wide * wide, axis=-1, keepdims=True) + EPS) * norm_gain
    return scaled.astype(jnp.bfloat16)


def finish(proj, positions, key_gain, kv_heads, head_size):
    shaped = proj.reshape(proj.shape[0], kv_heads, 2, head_size)
    raw_keys = shaped[:, :, 0]
    raw_keys = (
        raw_keys * lax.rsqrt(jnp.mean(raw_keys * raw_keys, axis=-1, keepdims=True) + EPS) * key_gain
    )
    keys = rotate(raw_keys, positions).astype(jnp.bfloat16)
    values = shaped[:, :, 1].astype(jnp.bfloat16)
    return jnp.stack([keys, values], axis=2).reshape(proj.shape[0], kv_heads * 2 * head_size)


def spread(hidden, block_owner, norm_gain, kv_weight, key_gain, queries, query_pos):
    n_ctx = lax.axis_size("ctx")
    n_hst = lax.axis_size("hst")
    n_head = lax.axis_size("head")
    src_dev, rows_blk, width = hidden.shape
    head_size = key_gain.shape[0]
    kv_dev = kv_weight.shape[1] // (2 * head_size)
    kv_all = kv_dev * n_hst
    q_dev = queries.shape[1] // head_size
    group = q_dev * n_hst * n_head // kv_all
    used = max(1, q_dev // group)
    q_rows = queries.shape[0]
    ctx_i = lax.axis_index("ctx")
    hst_i = lax.axis_index("hst")
    core_i = lax.axis_index("head")
    owner = block_owner[:, 0]
    n_blk = owner.shape[0]
    code = owner * n_blk + jnp.arange(n_blk, dtype=jnp.int32)
    starts = jnp.sum((code[None, :] < code[:, None]).astype(jnp.int32), axis=1) * rows_blk
    key_pos = (starts[:, None] + jnp.arange(rows_blk, dtype=jnp.int32)[None, :]).reshape(
        n_ctx, n_hst, n_head, src_dev * rows_blk
    )
    normed = normalize(hidden.reshape(src_dev * rows_blk, width), norm_gain)
    gathered = lax.all_gather(normed, "hst", axis=0, tiled=True)
    proj = jnp.dot(gathered, kv_weight, preferred_element_type=jnp.float32)
    my_pos = lax.dynamic_index_in_dim(
        lax.dynamic_index_in_dim(key_pos, ctx_i, 0, keepdims=False), core_i, 1, keepdims=False
    ).reshape(-1)
    restored = finish(proj, my_pos, key_gain, kv_dev, head_size)
    rows = restored.shape[0]
    by_head = restored.reshape(rows, kv_dev, 2 * head_size)
    parts = [
        lax.dynamic_slice_in_dim(
            by_head, (hst_i * n_head + c) * q_dev // group - hst_i * kv_dev, used, 1
        )
        for c in range(n_head)
    ]
    mine = lax.all_to_all(jnp.stack(parts), "head", split_axis=0, concat_axis=0, tiled=True)
    full = lax.all_gather(mine.reshape(n_head * rows, used * 2 * head_size), "ctx", axis=0, tiled=True)
    full = full.reshape(-1, used, 2, head_size)
    k_pos = jnp.transpose(key_pos, (0, 2, 1, 3)).reshape(-1)
    rotated = rotate(
        queries.astype(jnp.float32).reshape(q_rows, q_dev, head_size), query_pos
    ).astype(jnp.bfloat16)
    rotated = rotated.reshape(q_rows, used, q_dev // used, head_size)
    scores = jnp.einsum(
        "qagd,kad->agqk", rotated, full[:, :, 0], preferred_element_type=jnp.float32
    ) * (1.0 / math.sqrt(head_size))
    allowed = (k_pos[None, :] <= query_pos[:, None])[None, None]
    kept = jnp.where(allowed, scores, -1e30)
    best = jnp.max(kept, axis=-1, keepdims=True)
    weights = jnp.where(allowed, jnp.exp(kept - best), 0.0)
    total = jnp.sum(weights, axis=-1, keepdims=True)
    mixed = jnp.einsum(
        "agqk,kad->agqd", weights.astype(jnp.bfloat16), full[:, :, 1], preferred_element_type=jnp.float32
    )
    result = mixed / total
    return (
        jnp.transpose(result, (2, 0, 1, 3)).reshape(q_rows, q_dev * head_size).astype(jnp.bfloat16)
    )


def log2_of(value):
    return value.bit_length() - 1


def fused(
    dims, hid_ref, own_hbm, gain_hbm, w_ref, kgain_hbm, q_hbm, qpos_hbm, freq_hbm, out_ref,
    own_ref, gain_ref, kgain_ref, q_ref, qpos_ref, freq_ref, w_v, own_rows, peer_rows, kv_send, kv_buf, q_rot, q_turn, qpos_s, kpos_s, cos_s, sin_s,
    best, total, acc, w_sem, own_sem, small_sem, hid_send, hid_recv, send_sem, recv_sem, pair_sem, plane_sem,
):
    n_ctx, n_hst, n_head, src_dev, rows_blk, chunks = dims
    rows, width = own_rows.shape
    head_size = kgain_ref.shape[1]
    half = head_size // 2
    n_blk = own_ref.shape[1]
    n_src = n_ctx * n_head
    n_chunk = len(chunks)
    firsts = [sum(chunks[:j]) for j in range(n_chunk)]
    q_rows = q_ref.shape[0]
    q_dev = q_ref.shape[1] // head_size
    z = lax.axis_index("ctx")
    x = lax.axis_index("hst")
    c = lax.axis_index("head")
    me = z * n_head + c
    peer = 1 - x
    f32 = jnp.float32

    order = []
    for k in range(n_ctx - 1):
        up = k + (k >= z).astype(jnp.int32)
        down = n_ctx - 1 - k - (n_ctx - 1 - k <= z).astype(jnp.int32)
        stop = jnp.where(2 * z >= n_ctx, up, down)
        order.append((stop, lax.rem(stop - z + n_ctx, n_ctx)))
    targets = []
    for stop, dz in order:
        for core in range(n_head):
            targets.append(({"ctx": stop, "head": core}, core, (dz - 1) * n_head + c))
    for dc in range(1, n_head):
        core = lax.rem(c + dc, n_head)
        targets.append(({"head": core}, core, (n_ctx - 1) * n_head))

    barrier = pltpu.get_barrier_semaphore()

    @pl.when(x == 0)
    def _():
        pl.semaphore_signal(barrier, inc=1, device_id={"hst": peer}, device_id_type=MESH)

    own_copy = pltpu.make_async_copy(hid_ref, own_rows, own_sem)
    own_copy.start()
    small = [
        pltpu.make_async_copy(src, dst, small_sem.at[i])
        for i, (src, dst) in enumerate(
            [
                (own_hbm, own_ref),
                (freq_hbm, freq_ref),
                (gain_hbm, gain_ref),
                (kgain_hbm, kgain_ref),
                (qpos_hbm, qpos_ref),
                (q_hbm, q_ref),
            ]
        )
    ]
    small[2].start()

    def hidden_copy(j, part=None):
        rows_j = pl.ds(firsts[j], chunks[j])
        if j == 0:
            src, dst, sem = hid_ref.at[rows_j], peer_rows.at[rows_j], 0
        elif part is None:
            src, dst, sem = own_rows.at[rows_j], peer_rows.at[rows_j], j
        else:
            columns = pl.ds(part * (width // SLICES), width // SLICES)
            src, dst, sem = own_rows.at[rows_j, columns], peer_rows.at[rows_j, columns], j + part
        return pltpu.make_async_remote_copy(
            src_ref=src,
            dst_ref=dst,
            send_sem=hid_send.at[sem],
            recv_sem=hid_recv.at[sem],
            device_id={"hst": peer},
            device_id_type=MESH,
        )

    hidden_copies = [hidden_copy(j) for j in range(n_chunk - 1)]
    hidden_copies += [hidden_copy(n_chunk - 1, part) for part in range(SLICES)]

    @pl.when(x == 0)
    def _():
        pl.semaphore_wait(pair_sem, 1)

    @pl.when(x != 0)
    def _():
        pl.semaphore_wait(barrier, 1)
        pl.semaphore_signal(pair_sem, inc=1, device_id={"hst": peer}, device_id_type=MESH)

    hidden_copies[0].start()

    @pl.when(x == 0)
    def _():
        for device, _, _ in targets:
            pl.semaphore_signal(barrier, inc=1, device_id=device, device_id_type=MESH)

    def plane_ready():
        @pl.when(x == 0)
        def _():
            pl.semaphore_wait(barrier, len(targets))
            pl.semaphore_signal(plane_sem, inc=1, device_id={"hst": peer}, device_id_type=MESH)

        @pl.when(x != 0)
        def _():
            pl.semaphore_wait(plane_sem, 1)

    w_copy = pltpu.make_async_copy(w_ref, w_v, w_sem)
    for i in (0, 1, 3):
        small[i].start()
    w_copy.start()
    for i in (4, 5):
        small[i].start()

    def normed(raw):
        wide = raw.astype(f32)
        mean = jnp.mean(wide * wide, axis=-1, keepdims=True)
        return (wide * lax.rsqrt(mean + EPS) * gain_ref[...]).astype(jnp.bfloat16)

    small[2].wait()
    own_copy.wait()
    for j in range(1, n_chunk):
        part = slice(firsts[j], firsts[j] + chunks[j])
        own_rows[part] = normed(own_rows[part])
        for copy in hidden_copies[j:] if j == n_chunk - 1 else hidden_copies[j : j + 1]:
            copy.start()
    own_rows[0 : chunks[0]] = normed(own_rows[0 : chunks[0]])

    lane = lax.broadcasted_iota(jnp.int32, (n_blk, n_blk), 1)
    sub = lax.broadcasted_iota(jnp.int32, (n_blk, n_blk), 0)
    for copy in small[:2]:
        copy.wait()
    code_row = (own_ref[...] * n_blk + lane[0:1]).astype(f32)
    code_col = jnp.sum(jnp.where(sub == lane, code_row, 0.0), axis=1, keepdims=True)
    start_col = jnp.sum(jnp.where(code_row < code_col, float(rows_blk), 0.0), axis=1, keepdims=True)
    start_row = jnp.sum(jnp.where(code_col < code_row, float(rows_blk), 0.0), axis=0, keepdims=True)

    blk_bits = log2_of(rows_blk)
    freq = freq_ref[...]
    for side in range(2):
        source = x if side == 0 else peer
        base = ((z * n_hst + source) * n_head + c) * src_dev
        r = lax.broadcasted_iota(jnp.int32, (rows, n_blk), 0)
        hit = lax.broadcasted_iota(jnp.int32, (rows, n_blk), 1) == base + (r >> blk_bits)
        pos = jnp.sum(jnp.where(hit, start_row, 0.0), axis=1, keepdims=True)
        pos = pos + (r[:, 0:1] & (rows_blk - 1)).astype(f32)
        angle = pos * freq
        low = lax.broadcasted_iota(jnp.int32, angle.shape, 1) < half
        sine = jnp.sin(angle)
        cos_s[side * rows : (side + 1) * rows] = jnp.cos(angle)
        sin_s[side * rows : (side + 1) * rows] = jnp.where(low, -sine, sine)

    def turned(u, cosine, sine):
        return u * cosine + pltpu.roll(u, half, 1) * sine

    def kv_copy(row0, count, sem_row, device, core, slot, sem_col):
        return pltpu.make_async_remote_copy(
            src_ref=kv_send.at[core, pl.ds(row0, count)],
            dst_ref=kv_buf.at[slot, pl.ds(row0, count)],
            send_sem=send_sem.at[sem_row, sem_col],
            recv_sem=recv_sem.at[sem_row, sem_col],
            device_id=device,
            device_id_type=MESH,
        )

    def finish(proj, row0, count, stage):
        cosine = cos_s[row0 : row0 + count]
        sine = sin_s[row0 : row0 + count]
        kept = None
        for head in range(n_head):
            at = head * 2 * head_size
            raw = proj[:, at : at + head_size]
            scale = lax.rsqrt(jnp.mean(raw * raw, axis=-1, keepdims=True) + EPS)
            keys = turned(raw * scale * kgain_ref[...], cosine, sine).astype(jnp.bfloat16)
            values = proj[:, at + head_size : at + 2 * head_size].astype(jnp.bfloat16)
            both = jnp.concatenate([keys, values], axis=1)
            kv_send[head, row0 : row0 + count] = both
            kept = both if kept is None else jnp.where(c == head, both, kept)
        kv_buf[me, row0 : row0 + count] = kept
        if stage == 0:
            plane_ready()
        for device, core, sem_col in targets:
            kv_copy(row0, count, stage, device, core, me, sem_col).start()

    def project(rows_in, first=0, depth=None):
        depth = width if depth is None else depth
        return jnp.dot(rows_in, w_v[first : first + depth], preferred_element_type=f32)

    small[3].wait()
    w_copy.wait()
    finish(project(own_rows[...]), 0, rows, 0)

    r = lax.broadcasted_iota(jnp.int32, (rows, n_blk), 0)
    for side in range(2):
        source = x if side == 0 else peer
        for s in range(n_src):
            base = (((s // n_head) * n_hst + source) * n_head + s % n_head) * src_dev
            hit = lax.broadcasted_iota(jnp.int32, (rows, n_blk), 1) == base + (r >> blk_bits)
            pos = jnp.sum(jnp.where(hit, start_row, 0.0), axis=1, keepdims=True)
            pos = pos + (r[:, 0:1] & (rows_blk - 1)).astype(f32)
            for _, row0, count, _, _ in PLAN:
                if row0 // rows == side:
                    first = n_src * row0 + s * count
                    kpos_s[first : first + count] = pos[row0 % rows : row0 % rows + count]

    for copy in small[4:]:
        copy.wait()
    row = lax.broadcasted_iota(jnp.int32, (q_rows, q_rows), 0)
    column = lax.broadcasted_iota(jnp.int32, (q_rows, q_rows), 1)
    qpos = jnp.where(row == column, qpos_ref[...].astype(f32), 0.0)
    qpos = jnp.sum(qpos, axis=1, keepdims=True)
    q_angle = qpos * freq
    q_sine = jnp.sin(q_angle)
    low = lax.broadcasted_iota(jnp.int32, q_angle.shape, 1) < half
    q_sine = jnp.where(low, -q_sine, q_sine)
    q_cosine = jnp.cos(q_angle)
    for head in range(q_dev):
        u = q_ref[:, head * head_size : (head + 1) * head_size].astype(f32)
        q_rot[head * q_rows : (head + 1) * q_rows] = turned(u, q_cosine, q_sine)
    q_turn[...] = q_rot[...].T.astype(jnp.bfloat16)
    qpos_row = qpos_ref[...].astype(f32)
    qpos_s[...] = jnp.concatenate([qpos_row] * q_dev, axis=1)
    best[...] = jnp.full_like(best, -1e30)
    total[...] = jnp.zeros_like(total)
    acc[...] = jnp.zeros_like(acc)
    factor = math.log2(math.e) / math.sqrt(head_size)

    def attend(row0, count, tiles, step):
        at = n_src * row0
        span = n_src * count
        tile = tiles * q_rows
        step = min(step, span)
        keys = kv_buf[:, row0 : row0 + count, 0:head_size].reshape(span, head_size)
        values = kv_buf[:, row0 : row0 + count, head_size : 2 * head_size].reshape(span, head_size)

        def block(i, carry):
            part = pl.ds(pl.multiple_of(i * tile, tile), tile)
            q_part = q_turn[:, part]
            qpos_part = qpos_s[:, part]
            top, denom, mix = best[:, part], total[:, part], acc[:, part]
            for first in range(0, span, step):
                scores = jnp.dot(keys[first : first + step], q_part, preferred_element_type=f32)
                kpos = kpos_s[at + first : at + first + step]
                kept = jnp.where(kpos <= qpos_part, scores, -2e30)
                new = jnp.maximum(top, jnp.max(kept, axis=0, keepdims=True))
                weights = jnp.exp2((kept - new) * factor)
                fade = jnp.exp2((top - new) * factor)
                top = new
                denom = denom * fade + jnp.sum(weights, axis=0, keepdims=True)
                mix = mix * fade + lax.dot_general(
                    values[first : first + step],
                    weights.astype(jnp.bfloat16),
                    (((0,), (0,)), ((), ())),
                    preferred_element_type=f32,
                )
            best[:, part] = top
            total[:, part] = denom
            acc[:, part] = mix
            return carry

        lax.fori_loop(0, q_dev * q_rows // tile, block, 0)

    def arrive(row0, count, stage):
        for dz in range(1, n_ctx):
            for core in range(n_head):
                slot = lax.rem(z + n_ctx - dz, n_ctx) * n_head + core
                kv_copy(
                    row0, count, stage, targets[0][0], 0, slot, (dz - 1) * n_head + core
                ).wait_recv()
        for dc in range(1, n_head):
            slot = z * n_head + lax.rem(c + n_head - dc, n_head)
            kv_copy(
                row0, count, stage, targets[0][0], 0, slot, (n_ctx - 1) * n_head
            ).wait_recv()

    spans = [(0, rows)] + [(rows + firsts[j], chunks[j]) for j in range(n_chunk)]
    for stage in range(1, n_chunk + 1):
        part = slice(firsts[stage - 1], firsts[stage - 1] + chunks[stage - 1])
        if stage < n_chunk:
            hidden_copies[stage - 1].wait_recv()
            arrived = peer_rows[part]
            proj = project(normed(arrived) if stage == 1 else arrived)
        else:
            proj = None
            for i in range(SLICES):
                hidden_copies[stage - 1 + i].wait_recv()
                depth = width // SLICES
                term = project(peer_rows[part, i * depth : (i + 1) * depth], i * depth, depth)
                proj = term if proj is None else proj + term
        finish(proj, *spans[stage], stage)
        for after, row0, count, tiles, step in PLAN:
            if after == stage:
                for i, (first, size) in enumerate(spans):
                    if row0 <= first < row0 + count:
                        arrive(first, size, i)
                attend(row0, count, tiles, step)

    result = (acc[...] / total[...]).T
    for head in range(q_dev):
        out_ref[:, head * head_size : (head + 1) * head_size] = result[
            head * q_rows : (head + 1) * q_rows
        ].astype(out_ref.dtype)
    for copy in hidden_copies:
        copy.wait_send()
    for stage, (row0, count) in enumerate(spans):
        for device, core, sem_col in targets:
            kv_copy(row0, count, stage, device, core, me, sem_col).wait_send()


def body(hidden, block_owner, norm_gain, kv_weight, key_gain, queries, query_pos):
    n_ctx = lax.axis_size("ctx")
    n_hst = lax.axis_size("hst")
    n_head = lax.axis_size("head")
    src_dev, rows_blk, width = hidden.shape
    head_size = key_gain.shape[0]
    kv_dev = kv_weight.shape[1] // (2 * head_size)
    q_rows = queries.shape[0]
    q_dev = queries.shape[1] // head_size
    if n_hst != 2 or kv_dev != n_head or n_ctx > 4 or src_dev * rows_blk != sum(CHUNKS):
        return spread(hidden, block_owner, norm_gain, kv_weight, key_gain, queries, query_pos)
    rows = src_dev * rows_blk
    n_chunk = len(CHUNKS)
    n_src = n_ctx * n_head
    n_peer = n_src - 1
    half = head_size // 2
    freq = THETA ** (-(np.arange(half, dtype=np.float64) * 2.0) / head_size)
    freq = jnp.asarray(np.concatenate([freq, freq]).astype(np.float32)[None])
    vmem = pl.BlockSpec(memory_space=pltpu.VMEM)
    hbm = pl.BlockSpec(memory_space=pltpu.HBM)
    bf16, f32 = jnp.bfloat16, jnp.float32
    return pl.pallas_call(
        functools.partial(fused, (n_ctx, n_hst, n_head, src_dev, rows_blk, CHUNKS)),
        out_shape=jax.ShapeDtypeStruct(queries.shape, bf16),
        in_specs=[hbm] * 8,
        out_specs=vmem,
        scratch_shapes=[
            pltpu.VMEM((1, block_owner.shape[0]), jnp.int32),
            pltpu.VMEM((1, width), f32),
            pltpu.VMEM((1, head_size), f32),
            pltpu.VMEM(queries.shape, bf16),
            pltpu.VMEM((1, q_rows), jnp.int32),
            pltpu.VMEM((1, head_size), f32),
            pltpu.VMEM(kv_weight.shape, bf16),
            pltpu.VMEM((rows, width), bf16),
            pltpu.VMEM((rows, width), bf16),
            pltpu.VMEM((n_head, 2 * rows, 2 * head_size), bf16),
            pltpu.VMEM((n_src, 2 * rows, 2 * head_size), bf16),
            pltpu.VMEM((q_dev * q_rows, head_size), f32),
            pltpu.VMEM((head_size, q_dev * q_rows), bf16),
            pltpu.VMEM((1, q_dev * q_rows), f32),
            pltpu.VMEM((n_src * 2 * rows, 1), f32),
            pltpu.VMEM((2 * rows, head_size), f32),
            pltpu.VMEM((2 * rows, head_size), f32),
            pltpu.VMEM((1, q_dev * q_rows), f32),
            pltpu.VMEM((1, q_dev * q_rows), f32),
            pltpu.VMEM((head_size, q_dev * q_rows), f32),
            pltpu.SemaphoreType.DMA,
            pltpu.SemaphoreType.DMA,
            pltpu.SemaphoreType.DMA((6,)),
            pltpu.SemaphoreType.DMA((n_chunk - 1 + SLICES,)),
            pltpu.SemaphoreType.DMA((n_chunk - 1 + SLICES,)),
            pltpu.SemaphoreType.DMA((n_chunk + 1, n_peer)),
            pltpu.SemaphoreType.DMA((n_chunk + 1, n_peer)),
            pltpu.SemaphoreType.REGULAR,
            pltpu.SemaphoreType.REGULAR,
        ],
        compiler_params=pltpu.CompilerParams(
            collective_id=0, has_side_effects=True, vmem_limit_bytes=VMEM_LIMIT
        ),
    )(
        *[
            pltpu.with_memory_space_constraint(array, pltpu.HBM)
            for array in (
                hidden.reshape(rows, width),
                block_owner.reshape(1, -1),
                norm_gain[None],
                kv_weight,
                key_gain[None],
                queries,
                query_pos[None],
                freq,
            )
        ]
    )


def solution(mesh):
    in_specs = (
        P(("groups", "ctx", "hst", "head"), None, None),
        P("groups", None),
        P(),
        P(None, "hst"),
        P(),
        P(("groups", "ctx"), ("hst", "head")),
        P(("groups", "ctx")),
    )
    out_specs = P(("groups", "ctx"), ("hst", "head"))
    return jax.shard_map(body, mesh=mesh, in_specs=in_specs, out_specs=out_specs, check_vma=False)
```

```python
import functools
import math

import jax
import jax.numpy as jnp
import numpy as np
from jax import lax
from jax.experimental import pallas as pl
from jax.experimental.pallas import tpu as pltpu
from jax.sharding import PartitionSpec as P

EPS = 1e-06
THETA = 1000000.0
CHUNKS = (80, 32, 16)
SLICES = 4
PLAN = ((1, 0, 128, 8, 512), (3, 128, 80, 8, 640), (3, 208, 32, 16, 256), (3, 240, 16, 16, 128))
VMEM_LIMIT = 40 * 2**20
MESH = pl.DeviceIdType.MESH


def rotate(values, positions):
    half = values.shape[-1] // 2
    freq = THETA ** (-(jnp.arange(half, dtype=jnp.float32) * 2.0) / values.shape[-1])
    angle = positions.astype(jnp.float32)[:, None, None] * freq[None, None, :]
    cosine = jnp.cos(angle)
    sine = jnp.sin(angle)
    first = values[..., :half]
    second = values[..., half:]
    return jnp.concatenate(
        [first * cosine - second * sine, second * cosine + first * sine], axis=-1
    )


def normalize(rows, norm_gain):
    wide = rows.astype(jnp.float32)
    scaled = wide * lax.rsqrt(jnp.mean(wide * wide, axis=-1, keepdims=True) + EPS) * norm_gain
    return scaled.astype(jnp.bfloat16)


def finish(proj, positions, key_gain, kv_heads, head_size):
    shaped = proj.reshape(proj.shape[0], kv_heads, 2, head_size)
    raw_keys = shaped[:, :, 0]
    raw_keys = (
        raw_keys * lax.rsqrt(jnp.mean(raw_keys * raw_keys, axis=-1, keepdims=True) + EPS) * key_gain
    )
    keys = rotate(raw_keys, positions).astype(jnp.bfloat16)
    values = shaped[:, :, 1].astype(jnp.bfloat16)
    return jnp.stack([keys, values], axis=2).reshape(proj.shape[0], kv_heads * 2 * head_size)


def spread(hidden, block_owner, norm_gain, kv_weight, key_gain, queries, query_pos):
    n_ctx = lax.axis_size("ctx")
    n_hst = lax.axis_size("hst")
    n_head = lax.axis_size("head")
    src_dev, rows_blk, width = hidden.shape
    head_size = key_gain.shape[0]
    kv_dev = kv_weight.shape[1] // (2 * head_size)
    kv_all = kv_dev * n_hst
    q_dev = queries.shape[1] // head_size
    group = q_dev * n_hst * n_head // kv_all
    used = max(1, q_dev // group)
    q_rows = queries.shape[0]
    ctx_i = lax.axis_index("ctx")
    hst_i = lax.axis_index("hst")
    core_i = lax.axis_index("head")
    owner = block_owner[:, 0]
    n_blk = owner.shape[0]
    code = owner * n_blk + jnp.arange(n_blk, dtype=jnp.int32)
    starts = jnp.sum((code[None, :] < code[:, None]).astype(jnp.int32), axis=1) * rows_blk
    key_pos = (starts[:, None] + jnp.arange(rows_blk, dtype=jnp.int32)[None, :]).reshape(
        n_ctx, n_hst, n_head, src_dev * rows_blk
    )
    normed = normalize(hidden.reshape(src_dev * rows_blk, width), norm_gain)
    gathered = lax.all_gather(normed, "hst", axis=0, tiled=True)
    proj = jnp.dot(gathered, kv_weight, preferred_element_type=jnp.float32)
    my_pos = lax.dynamic_index_in_dim(
        lax.dynamic_index_in_dim(key_pos, ctx_i, 0, keepdims=False), core_i, 1, keepdims=False
    ).reshape(-1)
    restored = finish(proj, my_pos, key_gain, kv_dev, head_size)
    rows = restored.shape[0]
    by_head = restored.reshape(rows, kv_dev, 2 * head_size)
    parts = [
        lax.dynamic_slice_in_dim(
            by_head, (hst_i * n_head + c) * q_dev // group - hst_i * kv_dev, used, 1
        )
        for c in range(n_head)
    ]
    mine = lax.all_to_all(jnp.stack(parts), "head", split_axis=0, concat_axis=0, tiled=True)
    full = lax.all_gather(mine.reshape(n_head * rows, used * 2 * head_size), "ctx", axis=0, tiled=True)
    full = full.reshape(-1, used, 2, head_size)
    k_pos = jnp.transpose(key_pos, (0, 2, 1, 3)).reshape(-1)
    rotated = rotate(
        queries.astype(jnp.float32).reshape(q_rows, q_dev, head_size), query_pos
    ).astype(jnp.bfloat16)
    rotated = rotated.reshape(q_rows, used, q_dev // used, head_size)
    scores = jnp.einsum(
        "qagd,kad->agqk", rotated, full[:, :, 0], preferred_element_type=jnp.float32
    ) * (1.0 / math.sqrt(head_size))
    allowed = (k_pos[None, :] <= query_pos[:, None])[None, None]
    kept = jnp.where(allowed, scores, -1e30)
    best = jnp.max(kept, axis=-1, keepdims=True)
    weights = jnp.where(allowed, jnp.exp(kept - best), 0.0)
    total = jnp.sum(weights, axis=-1, keepdims=True)
    mixed = jnp.einsum(
        "agqk,kad->agqd", weights.astype(jnp.bfloat16), full[:, :, 1], preferred_element_type=jnp.float32
    )
    result = mixed / total
    return (
        jnp.transpose(result, (2, 0, 1, 3)).reshape(q_rows, q_dev * head_size).astype(jnp.bfloat16)
    )


def log2_of(value):
    return value.bit_length() - 1


def fused(
    dims, hid_ref, own_hbm, gain_hbm, w_ref, kgain_hbm, q_hbm, qpos_hbm, freq_hbm, out_ref,
    own_ref, gain_ref, kgain_ref, q_ref, qpos_ref, freq_ref, w_v, own_rows, peer_rows, kv_send, kv_buf, q_rot, q_turn, qpos_s, kpos_s, cos_s, sin_s,
    best, total, acc, w_sem, own_sem, small_sem, hid_send, hid_recv, send_sem, recv_sem, pair_sem, plane_sem,
):
    n_ctx, n_hst, n_head, src_dev, rows_blk, chunks = dims
    rows, width = own_rows.shape
    head_size = kgain_ref.shape[1]
    half = head_size // 2
    n_blk = own_ref.shape[1]
    n_src = n_ctx * n_head
    n_chunk = len(chunks)
    firsts = [sum(chunks[:j]) for j in range(n_chunk)]
    q_rows = q_ref.shape[0]
    q_dev = q_ref.shape[1] // head_size
    z = lax.axis_index("ctx")
    x = lax.axis_index("hst")
    c = lax.axis_index("head")
    me = z * n_head + c
    peer = 1 - x
    f32 = jnp.float32

    barrier = pltpu.get_barrier_semaphore()

    @pl.when(x == 0)
    def _():
        pl.semaphore_signal(barrier, inc=1, device_id={"hst": peer}, device_id_type=MESH)

    order = []
    for k in range(n_ctx - 1):
        up = k + (k >= z).astype(jnp.int32)
        down = n_ctx - 1 - k - (n_ctx - 1 - k <= z).astype(jnp.int32)
        stop = jnp.where(2 * z >= n_ctx, up, down)
        order.append((stop, lax.rem(stop - z + n_ctx, n_ctx)))
    targets = []
    for stop, dz in order:
        for core in range(n_head):
            targets.append(({"ctx": stop, "head": core}, core, (dz - 1) * n_head + c))
    for dc in range(1, n_head):
        core = lax.rem(c + dc, n_head)
        targets.append(({"head": core}, core, (n_ctx - 1) * n_head))

    own_copy = pltpu.make_async_copy(hid_ref, own_rows, own_sem)
    own_copy.start()
    small = [
        pltpu.make_async_copy(src, dst, small_sem.at[i])
        for i, (src, dst) in enumerate(
            [
                (own_hbm, own_ref),
                (freq_hbm, freq_ref),
                (gain_hbm, gain_ref),
                (kgain_hbm, kgain_ref),
                (qpos_hbm, qpos_ref),
                (q_hbm, q_ref),
            ]
        )
    ]
    small[2].start()

    def hidden_copy(j, part=None):
        rows_j = pl.ds(firsts[j], chunks[j])
        if j == 0:
            src, dst, sem = hid_ref.at[rows_j], peer_rows.at[rows_j], 0
        elif part is None:
            src, dst, sem = own_rows.at[rows_j], peer_rows.at[rows_j], j
        else:
            columns = pl.ds(part * (width // SLICES), width // SLICES)
            src, dst, sem = own_rows.at[rows_j, columns], peer_rows.at[rows_j, columns], j + part
        return pltpu.make_async_remote_copy(
            src_ref=src,
            dst_ref=dst,
            send_sem=hid_send.at[sem],
            recv_sem=hid_recv.at[sem],
            device_id={"hst": peer},
            device_id_type=MESH,
        )

    hidden_copies = [hidden_copy(j) for j in range(n_chunk - 1)]
    hidden_copies += [hidden_copy(n_chunk - 1, part) for part in range(SLICES)]

    @pl.when(x == 0)
    def _():
        pl.semaphore_wait(pair_sem, 1)

    @pl.when(x != 0)
    def _():
        pl.semaphore_wait(barrier, 1)
        pl.semaphore_signal(pair_sem, inc=1, device_id={"hst": peer}, device_id_type=MESH)

    hidden_copies[0].start()

    @pl.when(x == 0)
    def _():
        for device, _, _ in targets:
            pl.semaphore_signal(barrier, inc=1, device_id=device, device_id_type=MESH)

    def plane_ready():
        @pl.when(x == 0)
        def _():
            pl.semaphore_wait(barrier, len(targets))
            pl.semaphore_signal(plane_sem, inc=1, device_id={"hst": peer}, device_id_type=MESH)

        @pl.when(x != 0)
        def _():
            pl.semaphore_wait(plane_sem, 1)

    w_copy = pltpu.make_async_copy(w_ref, w_v, w_sem)
    for i in (0, 1, 3):
        small[i].start()
    w_copy.start()
    for i in (4, 5):
        small[i].start()

    def normed(raw):
        wide = raw.astype(f32)
        mean = jnp.mean(wide * wide, axis=-1, keepdims=True)
        return (wide * lax.rsqrt(mean + EPS) * gain_ref[...]).astype(jnp.bfloat16)

    small[2].wait()
    own_copy.wait()
    for j in range(1, n_chunk):
        part = slice(firsts[j], firsts[j] + chunks[j])
        own_rows[part] = normed(own_rows[part])
        for copy in hidden_copies[j:] if j == n_chunk - 1 else hidden_copies[j : j + 1]:
            copy.start()
    own_rows[0 : chunks[0]] = normed(own_rows[0 : chunks[0]])

    lane = lax.broadcasted_iota(jnp.int32, (n_blk, n_blk), 1)
    sub = lax.broadcasted_iota(jnp.int32, (n_blk, n_blk), 0)
    for copy in small[:2]:
        copy.wait()
    code_row = (own_ref[...] * n_blk + lane[0:1]).astype(f32)
    code_col = jnp.sum(jnp.where(sub == lane, code_row, 0.0), axis=1, keepdims=True)
    start_col = jnp.sum(jnp.where(code_row < code_col, float(rows_blk), 0.0), axis=1, keepdims=True)
    start_row = jnp.sum(jnp.where(code_col < code_row, float(rows_blk), 0.0), axis=0, keepdims=True)

    blk_bits = log2_of(rows_blk)
    freq = freq_ref[...]
    for side in range(2):
        source = x if side == 0 else peer
        base = ((z * n_hst + source) * n_head + c) * src_dev
        r = lax.broadcasted_iota(jnp.int32, (rows, n_blk), 0)
        hit = lax.broadcasted_iota(jnp.int32, (rows, n_blk), 1) == base + (r >> blk_bits)
        pos = jnp.sum(jnp.where(hit, start_row, 0.0), axis=1, keepdims=True)
        pos = pos + (r[:, 0:1] & (rows_blk - 1)).astype(f32)
        angle = pos * freq
        low = lax.broadcasted_iota(jnp.int32, angle.shape, 1) < half
        sine = jnp.sin(angle)
        cos_s[side * rows : (side + 1) * rows] = jnp.cos(angle)
        sin_s[side * rows : (side + 1) * rows] = jnp.where(low, -sine, sine)

    def turned(u, cosine, sine):
        return u * cosine + pltpu.roll(u, half, 1) * sine

    def kv_copy(row0, count, sem_row, device, core, slot, sem_col):
        return pltpu.make_async_remote_copy(
            src_ref=kv_send.at[core, pl.ds(row0, count)],
            dst_ref=kv_buf.at[slot, pl.ds(row0, count)],
            send_sem=send_sem.at[sem_row, sem_col],
            recv_sem=recv_sem.at[sem_row, sem_col],
            device_id=device,
            device_id_type=MESH,
        )

    def finish(proj, row0, count, stage):
        cosine = cos_s[row0 : row0 + count]
        sine = sin_s[row0 : row0 + count]
        kept = None
        for head in range(n_head):
            at = head * 2 * head_size
            raw = proj[:, at : at + head_size]
            scale = lax.rsqrt(jnp.mean(raw * raw, axis=-1, keepdims=True) + EPS)
            keys = turned(raw * scale * kgain_ref[...], cosine, sine).astype(jnp.bfloat16)
            values = proj[:, at + head_size : at + 2 * head_size].astype(jnp.bfloat16)
            both = jnp.concatenate([keys, values], axis=1)
            kv_send[head, row0 : row0 + count] = both
            kept = both if kept is None else jnp.where(c == head, both, kept)
        kv_buf[me, row0 : row0 + count] = kept
        if stage == 0:
            plane_ready()
        for device, core, sem_col in targets:
            kv_copy(row0, count, stage, device, core, me, sem_col).start()

    def project(rows_in, first=0, depth=None):
        depth = width if depth is None else depth
        return jnp.dot(rows_in, w_v[first : first + depth], preferred_element_type=f32)

    small[3].wait()
    w_copy.wait()
    finish(project(own_rows[...]), 0, rows, 0)

    r = lax.broadcasted_iota(jnp.int32, (rows, n_blk), 0)
    for side in range(2):
        source = x if side == 0 else peer
        for s in range(n_src):
            base = (((s // n_head) * n_hst + source) * n_head + s % n_head) * src_dev
            hit = lax.broadcasted_iota(jnp.int32, (rows, n_blk), 1) == base + (r >> blk_bits)
            pos = jnp.sum(jnp.where(hit, start_row, 0.0), axis=1, keepdims=True)
            pos = pos + (r[:, 0:1] & (rows_blk - 1)).astype(f32)
            for _, row0, count, _, _ in PLAN:
                if row0 // rows == side:
                    first = n_src * row0 + s * count
                    kpos_s[first : first + count] = pos[row0 % rows : row0 % rows + count]

    for copy in small[4:]:
        copy.wait()
    row = lax.broadcasted_iota(jnp.int32, (q_rows, q_rows), 0)
    column = lax.broadcasted_iota(jnp.int32, (q_rows, q_rows), 1)
    qpos = jnp.where(row == column, qpos_ref[...].astype(f32), 0.0)
    qpos = jnp.sum(qpos, axis=1, keepdims=True)
    q_angle = qpos * freq
    q_sine = jnp.sin(q_angle)
    low = lax.broadcasted_iota(jnp.int32, q_angle.shape, 1) < half
    q_sine = jnp.where(low, -q_sine, q_sine)
    q_cosine = jnp.cos(q_angle)
    for head in range(q_dev):
        u = q_ref[:, head * head_size : (head + 1) * head_size].astype(f32)
        q_rot[head * q_rows : (head + 1) * q_rows] = turned(u, q_cosine, q_sine)
    q_turn[...] = q_rot[...].T.astype(jnp.bfloat16)
    qpos_row = qpos_ref[...].astype(f32)
    qpos_s[...] = jnp.concatenate([qpos_row] * q_dev, axis=1)
    best[...] = jnp.full_like(best, -1e30)
    total[...] = jnp.zeros_like(total)
    acc[...] = jnp.zeros_like(acc)
    factor = math.log2(math.e) / math.sqrt(head_size)

    def attend(row0, count, tiles, step):
        at = n_src * row0
        span = n_src * count
        tile = tiles * q_rows
        step = min(step, span)
        keys = kv_buf[:, row0 : row0 + count, 0:head_size].reshape(span, head_size)
        values = kv_buf[:, row0 : row0 + count, head_size : 2 * head_size].reshape(span, head_size)

        def block(i, carry):
            part = pl.ds(pl.multiple_of(i * tile, tile), tile)
            q_part = q_turn[:, part]
            qpos_part = qpos_s[:, part]
            top, denom, mix = best[:, part], total[:, part], acc[:, part]
            for first in range(0, span, step):
                scores = jnp.dot(keys[first : first + step], q_part, preferred_element_type=f32)
                kpos = kpos_s[at + first : at + first + step]
                kept = jnp.where(kpos <= qpos_part, scores, -2e30)
                new = jnp.maximum(top, jnp.max(kept, axis=0, keepdims=True))
                weights = jnp.exp2((kept - new) * factor)
                fade = jnp.exp2((top - new) * factor)
                top = new
                denom = denom * fade + jnp.sum(weights, axis=0, keepdims=True)
                mix = mix * fade + lax.dot_general(
                    values[first : first + step],
                    weights.astype(jnp.bfloat16),
                    (((0,), (0,)), ((), ())),
                    preferred_element_type=f32,
                )
            best[:, part] = top
            total[:, part] = denom
            acc[:, part] = mix
            return carry

        lax.fori_loop(0, q_dev * q_rows // tile, block, 0)

    def arrive(row0, count, stage):
        for dz in range(1, n_ctx):
            for core in range(n_head):
                slot = lax.rem(z + n_ctx - dz, n_ctx) * n_head + core
                kv_copy(
                    row0, count, stage, targets[0][0], 0, slot, (dz - 1) * n_head + core
                ).wait_recv()
        for dc in range(1, n_head):
            slot = z * n_head + lax.rem(c + n_head - dc, n_head)
            kv_copy(
                row0, count, stage, targets[0][0], 0, slot, (n_ctx - 1) * n_head
            ).wait_recv()

    spans = [(0, rows)] + [(rows + firsts[j], chunks[j]) for j in range(n_chunk)]
    for stage in range(1, n_chunk + 1):
        part = slice(firsts[stage - 1], firsts[stage - 1] + chunks[stage - 1])
        if stage < n_chunk:
            hidden_copies[stage - 1].wait_recv()
            arrived = peer_rows[part]
            proj = project(normed(arrived) if stage == 1 else arrived)
        else:
            proj = None
            for i in range(SLICES):
                hidden_copies[stage - 1 + i].wait_recv()
                depth = width // SLICES
                term = project(peer_rows[part, i * depth : (i + 1) * depth], i * depth, depth)
                proj = term if proj is None else proj + term
        finish(proj, *spans[stage], stage)
        for after, row0, count, tiles, step in PLAN:
            if after == stage:
                for i, (first, size) in enumerate(spans):
                    if row0 <= first < row0 + count:
                        arrive(first, size, i)
                attend(row0, count, tiles, step)

    result = (acc[...] / total[...]).T
    for head in range(q_dev):
        out_ref[:, head * head_size : (head + 1) * head_size] = result[
            head * q_rows : (head + 1) * q_rows
        ].astype(out_ref.dtype)
    for copy in hidden_copies:
        copy.wait_send()
    for stage, (row0, count) in enumerate(spans):
        for device, core, sem_col in targets:
            kv_copy(row0, count, stage, device, core, me, sem_col).wait_send()


def body(hidden, block_owner, norm_gain, kv_weight, key_gain, queries, query_pos):
    n_ctx = lax.axis_size("ctx")
    n_hst = lax.axis_size("hst")
    n_head = lax.axis_size("head")
    src_dev, rows_blk, width = hidden.shape
    head_size = key_gain.shape[0]
    kv_dev = kv_weight.shape[1] // (2 * head_size)
    q_rows = queries.shape[0]
    q_dev = queries.shape[1] // head_size
    if n_hst != 2 or kv_dev != n_head or n_ctx > 4 or src_dev * rows_blk != sum(CHUNKS):
        return spread(hidden, block_owner, norm_gain, kv_weight, key_gain, queries, query_pos)
    rows = src_dev * rows_blk
    n_chunk = len(CHUNKS)
    n_src = n_ctx * n_head
    n_peer = n_src - 1
    half = head_size // 2
    freq = THETA ** (-(np.arange(half, dtype=np.float64) * 2.0) / head_size)
    freq = jnp.asarray(np.concatenate([freq, freq]).astype(np.float32)[None])
    vmem = pl.BlockSpec(memory_space=pltpu.VMEM)
    hbm = pl.BlockSpec(memory_space=pltpu.HBM)
    bf16, f32 = jnp.bfloat16, jnp.float32
    return pl.pallas_call(
        functools.partial(fused, (n_ctx, n_hst, n_head, src_dev, rows_blk, CHUNKS)),
        out_shape=jax.ShapeDtypeStruct(queries.shape, bf16),
        in_specs=[hbm] * 8,
        out_specs=vmem,
        scratch_shapes=[
            pltpu.VMEM((1, block_owner.shape[0]), jnp.int32),
            pltpu.VMEM((1, width), f32),
            pltpu.VMEM((1, head_size), f32),
            pltpu.VMEM(queries.shape, bf16),
            pltpu.VMEM((1, q_rows), jnp.int32),
            pltpu.VMEM((1, head_size), f32),
            pltpu.VMEM(kv_weight.shape, bf16),
            pltpu.VMEM((rows, width), bf16),
            pltpu.VMEM((rows, width), bf16),
            pltpu.VMEM((n_head, 2 * rows, 2 * head_size), bf16),
            pltpu.VMEM((n_src, 2 * rows, 2 * head_size), bf16),
            pltpu.VMEM((q_dev * q_rows, head_size), f32),
            pltpu.VMEM((head_size, q_dev * q_rows), bf16),
            pltpu.VMEM((1, q_dev * q_rows), f32),
            pltpu.VMEM((n_src * 2 * rows, 1), f32),
            pltpu.VMEM((2 * rows, head_size), f32),
            pltpu.VMEM((2 * rows, head_size), f32),
            pltpu.VMEM((1, q_dev * q_rows), f32),
            pltpu.VMEM((1, q_dev * q_rows), f32),
            pltpu.VMEM((head_size, q_dev * q_rows), f32),
            pltpu.SemaphoreType.DMA,
            pltpu.SemaphoreType.DMA,
            pltpu.SemaphoreType.DMA((6,)),
            pltpu.SemaphoreType.DMA((n_chunk - 1 + SLICES,)),
            pltpu.SemaphoreType.DMA((n_chunk - 1 + SLICES,)),
            pltpu.SemaphoreType.DMA((n_chunk + 1, n_peer)),
            pltpu.SemaphoreType.DMA((n_chunk + 1, n_peer)),
            pltpu.SemaphoreType.REGULAR,
            pltpu.SemaphoreType.REGULAR,
        ],
        compiler_params=pltpu.CompilerParams(
            collective_id=0, has_side_effects=True, vmem_limit_bytes=VMEM_LIMIT
        ),
    )(
        *[
            pltpu.with_memory_space_constraint(array, pltpu.HBM)
            for array in (
                hidden.reshape(rows, width),
                block_owner.reshape(1, -1),
                norm_gain[None],
                kv_weight,
                key_gain[None],
                queries,
                query_pos[None],
                freq,
            )
        ]
    )


def solution(mesh):
    in_specs = (
        P(("groups", "ctx", "hst", "head"), None, None),
        P("groups", None),
        P(),
        P(None, "hst"),
        P(),
        P(("groups", "ctx"), ("hst", "head")),
        P(("groups", "ctx")),
    )
    out_specs = P(("groups", "ctx"), ("hst", "head"))
    return jax.shard_map(body, mesh=mesh, in_specs=in_specs, out_specs=out_specs, check_vma=False)
```

```python
import functools
import math

import jax
import jax.numpy as jnp
import numpy as np
from jax import lax
from jax.experimental import pallas as pl
from jax.experimental.pallas import tpu as pltpu
from jax.sharding import PartitionSpec as P

EPS = 1e-06
THETA = 1000000.0
CHUNKS = (48, 48, 16, 16)
SLICES = 2
PLAN = ((2, 0, 128, 8, 512), (4, 128, 48, 8, 384), (4, 176, 48, 8, 384), (4, 224, 16, 16, 128), (4, 240, 16, 16, 128))
VMEM_LIMIT = 40 * 2**20
MESH = pl.DeviceIdType.MESH


def rotate(values, positions):
    half = values.shape[-1] // 2
    freq = THETA ** (-(jnp.arange(half, dtype=jnp.float32) * 2.0) / values.shape[-1])
    angle = positions.astype(jnp.float32)[:, None, None] * freq[None, None, :]
    cosine = jnp.cos(angle)
    sine = jnp.sin(angle)
    first = values[..., :half]
    second = values[..., half:]
    return jnp.concatenate(
        [first * cosine - second * sine, second * cosine + first * sine], axis=-1
    )


def normalize(rows, norm_gain):
    wide = rows.astype(jnp.float32)
    scaled = wide * lax.rsqrt(jnp.mean(wide * wide, axis=-1, keepdims=True) + EPS) * norm_gain
    return scaled.astype(jnp.bfloat16)


def finish(proj, positions, key_gain, kv_heads, head_size):
    shaped = proj.reshape(proj.shape[0], kv_heads, 2, head_size)
    raw_keys = shaped[:, :, 0]
    raw_keys = (
        raw_keys * lax.rsqrt(jnp.mean(raw_keys * raw_keys, axis=-1, keepdims=True) + EPS) * key_gain
    )
    keys = rotate(raw_keys, positions).astype(jnp.bfloat16)
    values = shaped[:, :, 1].astype(jnp.bfloat16)
    return jnp.stack([keys, values], axis=2).reshape(proj.shape[0], kv_heads * 2 * head_size)


def spread(hidden, block_owner, norm_gain, kv_weight, key_gain, queries, query_pos):
    n_ctx = lax.axis_size("ctx")
    n_hst = lax.axis_size("hst")
    n_head = lax.axis_size("head")
    src_dev, rows_blk, width = hidden.shape
    head_size = key_gain.shape[0]
    kv_dev = kv_weight.shape[1] // (2 * head_size)
    kv_all = kv_dev * n_hst
    q_dev = queries.shape[1] // head_size
    group = q_dev * n_hst * n_head // kv_all
    used = max(1, q_dev // group)
    q_rows = queries.shape[0]
    ctx_i = lax.axis_index("ctx")
    hst_i = lax.axis_index("hst")
    core_i = lax.axis_index("head")
    owner = block_owner[:, 0]
    n_blk = owner.shape[0]
    code = owner * n_blk + jnp.arange(n_blk, dtype=jnp.int32)
    starts = jnp.sum((code[None, :] < code[:, None]).astype(jnp.int32), axis=1) * rows_blk
    key_pos = (starts[:, None] + jnp.arange(rows_blk, dtype=jnp.int32)[None, :]).reshape(
        n_ctx, n_hst, n_head, src_dev * rows_blk
    )
    normed = normalize(hidden.reshape(src_dev * rows_blk, width), norm_gain)
    gathered = lax.all_gather(normed, "hst", axis=0, tiled=True)
    proj = jnp.dot(gathered, kv_weight, preferred_element_type=jnp.float32)
    my_pos = lax.dynamic_index_in_dim(
        lax.dynamic_index_in_dim(key_pos, ctx_i, 0, keepdims=False), core_i, 1, keepdims=False
    ).reshape(-1)
    restored = finish(proj, my_pos, key_gain, kv_dev, head_size)
    rows = restored.shape[0]
    by_head = restored.reshape(rows, kv_dev, 2 * head_size)
    parts = [
        lax.dynamic_slice_in_dim(
            by_head, (hst_i * n_head + c) * q_dev // group - hst_i * kv_dev, used, 1
        )
        for c in range(n_head)
    ]
    mine = lax.all_to_all(jnp.stack(parts), "head", split_axis=0, concat_axis=0, tiled=True)
    full = lax.all_gather(mine.reshape(n_head * rows, used * 2 * head_size), "ctx", axis=0, tiled=True)
    full = full.reshape(-1, used, 2, head_size)
    k_pos = jnp.transpose(key_pos, (0, 2, 1, 3)).reshape(-1)
    rotated = rotate(
        queries.astype(jnp.float32).reshape(q_rows, q_dev, head_size), query_pos
    ).astype(jnp.bfloat16)
    rotated = rotated.reshape(q_rows, used, q_dev // used, head_size)
    scores = jnp.einsum(
        "qagd,kad->agqk", rotated, full[:, :, 0], preferred_element_type=jnp.float32
    ) * (1.0 / math.sqrt(head_size))
    allowed = (k_pos[None, :] <= query_pos[:, None])[None, None]
    kept = jnp.where(allowed, scores, -1e30)
    best = jnp.max(kept, axis=-1, keepdims=True)
    weights = jnp.where(allowed, jnp.exp(kept - best), 0.0)
    total = jnp.sum(weights, axis=-1, keepdims=True)
    mixed = jnp.einsum(
        "agqk,kad->agqd", weights.astype(jnp.bfloat16), full[:, :, 1], preferred_element_type=jnp.float32
    )
    result = mixed / total
    return (
        jnp.transpose(result, (2, 0, 1, 3)).reshape(q_rows, q_dev * head_size).astype(jnp.bfloat16)
    )


def log2_of(value):
    return value.bit_length() - 1


def fused(
    dims, hid_ref, own_hbm, gain_hbm, w_ref, kgain_hbm, q_hbm, qpos_hbm, freq_hbm, out_ref,
    own_ref, gain_ref, kgain_ref, q_ref, qpos_ref, freq_ref, w_v, own_rows, peer_rows, kv_send, kv_buf, q_rot, q_turn, qpos_s, kpos_s, cos_s, sin_s,
    best, total, acc, w_sem, own_sem, small_sem, hid_send, hid_recv, send_sem, recv_sem, plane_sem,
    moved_rows, moved_peer, moved_kv, moved_cos, moved_sin, moved_sem, moved_kv_send,
):
    n_ctx, n_hst, n_head, src_dev, rows_blk, chunks = dims
    rows, width = own_rows.shape
    head_size = kgain_ref.shape[1]
    half = head_size // 2
    n_blk = own_ref.shape[1]
    n_src = n_ctx * n_head
    n_chunk = len(chunks)
    firsts = [sum(chunks[:j]) for j in range(n_chunk)]
    q_rows = q_ref.shape[0]
    q_dev = q_ref.shape[1] // head_size
    z = lax.axis_index("ctx")
    x = lax.axis_index("hst")
    c = lax.axis_index("head")
    me = z * n_head + c
    peer = 1 - x
    f32 = jnp.float32
    giver_slot = (n_ctx - 1) * n_head
    giver = me == giver_slot
    keeper = me != giver_slot
    taker = me == n_head - 1
    late = n_chunk - 1
    late0, late_rows = firsts[late - 1], chunks[late - 1]
    last0, last_rows = firsts[-1], chunks[-1]

    barrier = pltpu.get_barrier_semaphore()

    pl.semaphore_signal(barrier, inc=1, device_id={"hst": peer}, device_id_type=MESH)
    head_of_plane = (n_ctx - 1) * n_head

    @pl.when(me != head_of_plane)
    def _():
        pl.semaphore_signal(
            barrier, inc=1, device_id={"ctx": n_ctx - 1, "head": 0}, device_id_type=MESH
        )

    order = []
    for k in range(n_ctx - 1):
        up = k + (k >= z).astype(jnp.int32)
        down = n_ctx - 1 - k - (n_ctx - 1 - k <= z).astype(jnp.int32)
        stop = jnp.where(2 * z >= n_ctx, up, down)
        order.append((stop, lax.rem(stop - z + n_ctx, n_ctx)))
    targets = []
    for stop, dz in order:
        for core in range(n_head):
            targets.append(({"ctx": stop, "head": core}, core, (dz - 1) * n_head + c))
    for dc in range(1, n_head):
        core = lax.rem(c + dc, n_head)
        targets.append(({"head": core}, core, (n_ctx - 1) * n_head))

    own_copy = pltpu.make_async_copy(hid_ref, own_rows, own_sem)
    own_copy.start()
    small = [
        pltpu.make_async_copy(src, dst, small_sem.at[i])
        for i, (src, dst) in enumerate(
            [
                (own_hbm, own_ref),
                (freq_hbm, freq_ref),
                (gain_hbm, gain_ref),
                (kgain_hbm, kgain_ref),
                (qpos_hbm, qpos_ref),
                (q_hbm, q_ref),
            ]
        )
    ]
    small[2].start()

    def hidden_copy(j, part=None):
        rows_j = pl.ds(firsts[j], chunks[j])
        if j == 0:
            src, dst, sem = hid_ref.at[rows_j], peer_rows.at[rows_j], 0
        elif part is None:
            src, dst, sem = own_rows.at[rows_j], peer_rows.at[rows_j], j
        else:
            columns = pl.ds(part * (width // SLICES), width // SLICES)
            src, dst, sem = own_rows.at[rows_j, columns], peer_rows.at[rows_j, columns], j + part
        return pltpu.make_async_remote_copy(
            src_ref=src,
            dst_ref=dst,
            send_sem=hid_send.at[sem],
            recv_sem=hid_recv.at[sem],
            device_id={"hst": peer},
            device_id_type=MESH,
        )

    hidden_copies = [hidden_copy(j) for j in range(n_chunk - 1)]
    last_copies = [hidden_copy(n_chunk - 1, part) for part in range(SLICES)]
    move = pltpu.make_async_remote_copy(
        src_ref=own_rows.at[pl.ds(late0, late_rows)],
        dst_ref=moved_rows,
        send_sem=moved_sem.at[0],
        recv_sem=moved_sem.at[1],
        device_id={"ctx": 0, "head": n_head - 1},
        device_id_type=MESH,
    )
    cross = pltpu.make_async_remote_copy(
        src_ref=moved_rows,
        dst_ref=moved_peer,
        send_sem=moved_sem.at[2],
        recv_sem=moved_sem.at[3],
        device_id={"hst": peer},
        device_id_type=MESH,
    )

    @pl.when(me != head_of_plane)
    def _():
        pl.semaphore_wait(barrier, 1)

    @pl.when(me == head_of_plane)
    def _():
        pl.semaphore_wait(barrier, n_src)

    hidden_copies[0].start()

    @pl.when(me == head_of_plane)
    def _():
        for stop in range(n_ctx):
            for core in range(n_head):
                if stop * n_head + core != head_of_plane:
                    device = {"ctx": stop, "head": core}
                    pl.semaphore_signal(plane_sem, inc=1, device_id=device, device_id_type=MESH)

    def plane_ready():
        @pl.when(me != head_of_plane)
        def _():
            pl.semaphore_wait(plane_sem, 1)

    w_copy = pltpu.make_async_copy(w_ref, w_v, w_sem)
    for i in (0, 1, 3):
        small[i].start()
    w_copy.start()
    for i in (4, 5):
        small[i].start()

    def normed(raw):
        wide = raw.astype(f32)
        mean = jnp.mean(wide * wide, axis=-1, keepdims=True)
        return (wide * lax.rsqrt(mean + EPS) * gain_ref[...]).astype(jnp.bfloat16)

    small[2].wait()
    own_copy.wait()
    for j in range(1, n_chunk):
        part = slice(firsts[j], firsts[j] + chunks[j])
        own_rows[part] = normed(own_rows[part])
        if j < late - 1:
            hidden_copies[j].start()
        elif j == late - 1:
            pl.when(keeper)(hidden_copies[j].start)
            pl.when(giver)(move.start)

    @pl.when(jnp.logical_not(taker))
    def _():
        for copy in last_copies:
            copy.start()

    own_rows[0 : chunks[0]] = normed(own_rows[0 : chunks[0]])

    lane = lax.broadcasted_iota(jnp.int32, (n_blk, n_blk), 1)
    sub = lax.broadcasted_iota(jnp.int32, (n_blk, n_blk), 0)
    for copy in small[:2]:
        copy.wait()
    code_row = (own_ref[...] * n_blk + lane[0:1]).astype(f32)
    code_col = jnp.sum(jnp.where(sub == lane, code_row, 0.0), axis=1, keepdims=True)
    start_col = jnp.sum(jnp.where(code_row < code_col, float(rows_blk), 0.0), axis=1, keepdims=True)
    start_row = jnp.sum(jnp.where(code_col < code_row, float(rows_blk), 0.0), axis=0, keepdims=True)

    blk_bits = log2_of(rows_blk)
    freq = freq_ref[...]
    def turns(base, row0, count):
        r = row0 + lax.broadcasted_iota(jnp.int32, (count, n_blk), 0)
        hit = lax.broadcasted_iota(jnp.int32, (count, n_blk), 1) == base + (r >> blk_bits)
        pos = jnp.sum(jnp.where(hit, start_row, 0.0), axis=1, keepdims=True)
        angle = (pos + (r[:, 0:1] & (rows_blk - 1)).astype(f32)) * freq
        low = lax.broadcasted_iota(jnp.int32, angle.shape, 1) < half
        sine = jnp.sin(angle)
        return jnp.cos(angle), jnp.where(low, -sine, sine)

    for side in range(2):
        source = x if side == 0 else peer
        base = ((z * n_hst + source) * n_head + c) * src_dev
        cosine, sine = turns(base, 0, rows)
        cos_s[side * rows : (side + 1) * rows] = cosine
        sin_s[side * rows : (side + 1) * rows] = sine

    @pl.when(taker)
    def _():
        base = ((n_ctx - 1) * n_hst + peer) * n_head * src_dev
        cosine, sine = turns(base, late0, late_rows)
        moved_cos[...] = cosine
        moved_sin[...] = sine

    def turned(u, cosine, sine):
        return u * cosine + pltpu.roll(u, half, 1) * sine

    def kv_copy(row0, count, sem_row, device, core, slot, sem_col):
        return pltpu.make_async_remote_copy(
            src_ref=kv_send.at[core, pl.ds(row0, count)],
            dst_ref=kv_buf.at[slot, pl.ds(row0, count)],
            send_sem=send_sem.at[sem_row, sem_col],
            recv_sem=recv_sem.at[sem_row, sem_col],
            device_id=device,
            device_id_type=MESH,
        )

    def keys_values(proj, cosine, sine):
        pairs = []
        for head in range(n_head):
            at = head * 2 * head_size
            raw = proj[:, at : at + head_size]
            scale = lax.rsqrt(jnp.mean(raw * raw, axis=-1, keepdims=True) + EPS)
            keys = turned(raw * scale * kgain_ref[...], cosine, sine).astype(jnp.bfloat16)
            values = proj[:, at + head_size : at + 2 * head_size].astype(jnp.bfloat16)
            pairs.append(jnp.concatenate([keys, values], axis=1))
        return pairs

    def finish(proj, row0, count, stage):
        pairs = keys_values(proj, cos_s[row0 : row0 + count], sin_s[row0 : row0 + count])
        kept = pairs[0]
        for head, both in enumerate(pairs):
            kv_send[head, row0 : row0 + count] = both
            kept = jnp.where(c == head, both, kept)
        kv_buf[me, row0 : row0 + count] = kept
        if stage == 0:
            plane_ready()
        for device, core, sem_col in targets:
            kv_copy(row0, count, stage, device, core, me, sem_col).start()

    moved_kv_copies = []
    for stop in range(n_ctx - 1, -1, -1):
        for core in range(n_head if stop else n_head - 1):
            sem_col = stop * n_head if stop < n_ctx - 1 else giver_slot + n_head - 1 - core
            moved_kv_copies.append(
                pltpu.make_async_remote_copy(
                    src_ref=moved_kv.at[core],
                    dst_ref=kv_buf.at[giver_slot, pl.ds(rows + late0, late_rows)],
                    send_sem=moved_kv_send.at[len(moved_kv_copies)],
                    recv_sem=recv_sem.at[late, sem_col],
                    device_id={"ctx": stop, "head": core},
                    device_id_type=MESH,
                )
            )

    def finish_moved(proj):
        pairs = keys_values(proj, moved_cos[...], moved_sin[...])
        for head, both in enumerate(pairs):
            moved_kv[head] = both
        kv_buf[giver_slot, rows + late0 : rows + late0 + late_rows] = pairs[n_head - 1]
        for copy in moved_kv_copies:
            copy.start()

    def project(rows_in, first=0, depth=None):
        depth = width if depth is None else depth
        return jnp.dot(rows_in, w_v[first : first + depth], preferred_element_type=f32)

    small[3].wait()
    w_copy.wait()
    finish(project(own_rows[...]), 0, rows, 0)

    r = lax.broadcasted_iota(jnp.int32, (rows, n_blk), 0)
    for side in range(2):
        source = x if side == 0 else peer
        for s in range(n_src):
            base = (((s // n_head) * n_hst + source) * n_head + s % n_head) * src_dev
            hit = lax.broadcasted_iota(jnp.int32, (rows, n_blk), 1) == base + (r >> blk_bits)
            pos = jnp.sum(jnp.where(hit, start_row, 0.0), axis=1, keepdims=True)
            pos = pos + (r[:, 0:1] & (rows_blk - 1)).astype(f32)
            for _, row0, count, _, _ in PLAN:
                if row0 // rows == side:
                    first = n_src * row0 + s * count
                    kpos_s[first : first + count] = pos[row0 % rows : row0 % rows + count]

    for copy in small[4:]:
        copy.wait()
    row = lax.broadcasted_iota(jnp.int32, (q_rows, q_rows), 0)
    column = lax.broadcasted_iota(jnp.int32, (q_rows, q_rows), 1)
    qpos = jnp.where(row == column, qpos_ref[...].astype(f32), 0.0)
    qpos = jnp.sum(qpos, axis=1, keepdims=True)
    q_angle = qpos * freq
    q_sine = jnp.sin(q_angle)
    low = lax.broadcasted_iota(jnp.int32, q_angle.shape, 1) < half
    q_sine = jnp.where(low, -q_sine, q_sine)
    q_cosine = jnp.cos(q_angle)
    for head in range(q_dev):
        u = q_ref[:, head * head_size : (head + 1) * head_size].astype(f32)
        q_rot[head * q_rows : (head + 1) * q_rows] = turned(u, q_cosine, q_sine)
    q_turn[...] = q_rot[...].T.astype(jnp.bfloat16)
    qpos_row = qpos_ref[...].astype(f32)
    qpos_s[...] = jnp.concatenate([qpos_row] * q_dev, axis=1)
    best[...] = jnp.full_like(best, -1e30)
    total[...] = jnp.zeros_like(total)
    acc[...] = jnp.zeros_like(acc)
    factor = math.log2(math.e) / math.sqrt(head_size)

    def put(mix, denom):
        result = (mix * (1.0 / denom)).T
        for head in range(q_dev):
            out_ref[:, head * head_size : (head + 1) * head_size] = result[
                head * q_rows : (head + 1) * q_rows
            ].astype(out_ref.dtype)

    def attend(row0, count, tiles, step, last):
        at = n_src * row0
        span = n_src * count
        tile = tiles * q_rows
        step = min(step, span)
        keys = kv_buf[:, row0 : row0 + count, 0:head_size].reshape(span, head_size)
        values = kv_buf[:, row0 : row0 + count, head_size : 2 * head_size].reshape(span, head_size)

        def block(i, carry):
            part = slice(None) if last else pl.ds(pl.multiple_of(i * tile, tile), tile)
            q_part = q_turn[:, part]
            qpos_part = qpos_s[:, part]
            top, denom, mix = best[:, part], total[:, part], acc[:, part]
            for first in range(0, span, step):
                scores = jnp.dot(keys[first : first + step], q_part, preferred_element_type=f32)
                kpos = kpos_s[at + first : at + first + step]
                kept = jnp.where(kpos <= qpos_part, scores, -2e30)
                new = jnp.maximum(top, jnp.max(kept, axis=0, keepdims=True))
                weights = jnp.exp2((kept - new) * factor)
                fade = jnp.exp2((top - new) * factor)
                top = new
                denom = denom * fade + jnp.sum(weights, axis=0, keepdims=True)
                mix = mix * fade + lax.dot_general(
                    values[first : first + step],
                    weights.astype(jnp.bfloat16),
                    (((0,), (0,)), ((), ())),
                    preferred_element_type=f32,
                )
            if last:
                put(mix, denom)
                return carry
            best[:, part] = top
            total[:, part] = denom
            acc[:, part] = mix
            return carry

        if last:
            block(0, 0)
        else:
            lax.fori_loop(0, q_dev * q_rows // tile, block, 0)

    def arrive(row0, count, stage):
        def one(slot, sem_col):
            kv_copy(row0, count, stage, targets[0][0], 0, slot, sem_col).wait_recv()

        for dz in range(1, n_ctx):
            for core in range(n_head):
                slot = lax.rem(z + n_ctx - dz, n_ctx) * n_head + core
                wait = functools.partial(one, slot, (dz - 1) * n_head + core)
                if stage == late and dz == 1 and core == 0:
                    pl.when(jnp.logical_not(taker))(wait)
                else:
                    wait()
        for dc in range(1, n_head):
            one(z * n_head + lax.rem(c + n_head - dc, n_head), giver_slot)
        if stage == late:
            pl.when(giver)(functools.partial(one, giver_slot, giver_slot + 1))

    def sliced(copies, rows_ref, row0, count):
        proj = None
        depth = width // SLICES
        for i, copy in enumerate(copies):
            copy.wait_recv()
            term = project(rows_ref[row0 : row0 + count, i * depth : (i + 1) * depth], i * depth, depth)
            proj = term if proj is None else proj + term
        return proj

    @pl.when(taker)
    def _():
        move.wait_recv()
        cross.start()
        for copy in last_copies:
            copy.start()

    spans = [(0, rows)] + [(rows + firsts[j], chunks[j]) for j in range(n_chunk)]
    for stage in range(1, n_chunk + 1):

        def restore(stage=stage):
            hidden_copies[stage - 1].wait_recv()
            arrived = peer_rows[firsts[stage - 1] : firsts[stage - 1] + chunks[stage - 1]]
            finish(project(normed(arrived) if stage == 1 else arrived), *spans[stage], stage)

        if stage == n_chunk:
            finish(sliced(last_copies, peer_rows, last0, last_rows), *spans[stage], stage)
        elif stage == late:
            pl.when(keeper)(restore)

            @pl.when(taker)
            def _():
                cross.wait_recv()
                finish_moved(project(moved_peer[...]))
        else:
            restore()

        for i_plan, (after, row0, count, tiles, step) in enumerate(PLAN):
            if after == stage:
                for i, (first, size) in enumerate(spans):
                    if row0 <= first < row0 + count:
                        arrive(first, size, i)
                attend(row0, count, tiles, step, i_plan == len(PLAN) - 1)

    def sent(stage):
        for device, core, sem_col in targets:
            kv_copy(*spans[stage], stage, device, core, me, sem_col).wait_send()

    def sent(stage):
        for device, core, sem_col in targets:
            kv_copy(*spans[stage], stage, device, core, me, sem_col).wait_send()

    for j, copy in enumerate(hidden_copies):
        if j != late - 1:
            copy.wait_send()
    for copy in last_copies:
        copy.wait_send()
    for stage in range(n_chunk + 1):
        if stage != late:
            sent(stage)

    @pl.when(keeper)
    def _():
        hidden_copies[late - 1].wait_send()
        sent(late)

    @pl.when(giver)
    def _():
        move.wait_send()

    @pl.when(taker)
    def _():
        for copy in [cross] + moved_kv_copies:
            copy.wait_send()


def body(hidden, block_owner, norm_gain, kv_weight, key_gain, queries, query_pos):
    n_ctx = lax.axis_size("ctx")
    n_hst = lax.axis_size("hst")
    n_head = lax.axis_size("head")
    src_dev, rows_blk, width = hidden.shape
    head_size = key_gain.shape[0]
    kv_dev = kv_weight.shape[1] // (2 * head_size)
    q_rows = queries.shape[0]
    q_dev = queries.shape[1] // head_size
    if n_hst != 2 or n_head != 2 or kv_dev != n_head or n_ctx not in (2, 4) or src_dev * rows_blk != sum(CHUNKS):
        return spread(hidden, block_owner, norm_gain, kv_weight, key_gain, queries, query_pos)
    rows = src_dev * rows_blk
    n_chunk = len(CHUNKS)
    n_src = n_ctx * n_head
    n_peer = n_src - 1
    half = head_size // 2
    freq = THETA ** (-(np.arange(half, dtype=np.float64) * 2.0) / head_size)
    freq = jnp.asarray(np.concatenate([freq, freq]).astype(np.float32)[None])
    vmem = pl.BlockSpec(memory_space=pltpu.VMEM)
    hbm = pl.BlockSpec(memory_space=pltpu.HBM)
    bf16, f32 = jnp.bfloat16, jnp.float32
    return pl.pallas_call(
        functools.partial(fused, (n_ctx, n_hst, n_head, src_dev, rows_blk, CHUNKS)),
        out_shape=jax.ShapeDtypeStruct(queries.shape, bf16),
        in_specs=[hbm] * 8,
        out_specs=vmem,
        scratch_shapes=[
            pltpu.VMEM((1, block_owner.shape[0]), jnp.int32),
            pltpu.VMEM((1, width), f32),
            pltpu.VMEM((1, head_size), f32),
            pltpu.VMEM(queries.shape, bf16),
            pltpu.VMEM((1, q_rows), jnp.int32),
            pltpu.VMEM((1, head_size), f32),
            pltpu.VMEM(kv_weight.shape, bf16),
            pltpu.VMEM((rows, width), bf16),
            pltpu.VMEM((rows, width), bf16),
            pltpu.VMEM((n_head, 2 * rows, 2 * head_size), bf16),
            pltpu.VMEM((n_src, 2 * rows, 2 * head_size), bf16),
            pltpu.VMEM((q_dev * q_rows, head_size), f32),
            pltpu.VMEM((head_size, q_dev * q_rows), bf16),
            pltpu.VMEM((1, q_dev * q_rows), f32),
            pltpu.VMEM((n_src * 2 * rows, 1), f32),
            pltpu.VMEM((2 * rows, head_size), f32),
            pltpu.VMEM((2 * rows, head_size), f32),
            pltpu.VMEM((1, q_dev * q_rows), f32),
            pltpu.VMEM((1, q_dev * q_rows), f32),
            pltpu.VMEM((head_size, q_dev * q_rows), f32),
            pltpu.SemaphoreType.DMA,
            pltpu.SemaphoreType.DMA,
            pltpu.SemaphoreType.DMA((6,)),
            pltpu.SemaphoreType.DMA((n_chunk - 1 + SLICES,)),
            pltpu.SemaphoreType.DMA((n_chunk - 1 + SLICES,)),
            pltpu.SemaphoreType.DMA((n_chunk + 1, n_peer)),
            pltpu.SemaphoreType.DMA((n_chunk + 1, n_peer + 1)),
            pltpu.SemaphoreType.REGULAR,
            pltpu.VMEM((CHUNKS[-2], width), bf16),
            pltpu.VMEM((CHUNKS[-2], width), bf16),
            pltpu.VMEM((n_head, CHUNKS[-2], 2 * head_size), bf16),
            pltpu.VMEM((CHUNKS[-2], head_size), f32),
            pltpu.VMEM((CHUNKS[-2], head_size), f32),
            pltpu.SemaphoreType.DMA((4,)),
            pltpu.SemaphoreType.DMA((n_peer,)),
        ],
        compiler_params=pltpu.CompilerParams(
            collective_id=0, has_side_effects=True, vmem_limit_bytes=VMEM_LIMIT
        ),
    )(
        *[
            pltpu.with_memory_space_constraint(array, pltpu.HBM)
            for array in (
                hidden.reshape(rows, width),
                block_owner.reshape(1, -1),
                norm_gain[None],
                kv_weight,
                key_gain[None],
                queries,
                query_pos[None],
                freq,
            )
        ]
    )


def solution(mesh):
    in_specs = (
        P(("groups", "ctx", "hst", "head"), None, None),
        P("groups", None),
        P(),
        P(None, "hst"),
        P(),
        P(("groups", "ctx"), ("hst", "head")),
        P(("groups", "ctx")),
    )
    out_specs = P(("groups", "ctx"), ("hst", "head"))
    return jax.shard_map(body, mesh=mesh, in_specs=in_specs, out_specs=out_specs, check_vma=False)
```

```python
import functools
import math

import jax
import jax.numpy as jnp
import numpy as np
from jax import lax
from jax.experimental import pallas as pl
from jax.experimental.pallas import tpu as pltpu
from jax.sharding import PartitionSpec as P

EPS = 1e-06
THETA = 1000000.0
CHUNKS = (64, 32, 16, 16)
SLICES = 2
PLAN = ((2, 0, 128, 8, 512), (4, 128, 64, 8, 512), (4, 192, 32, 16, 256), (4, 224, 16, 16, 128), (4, 240, 16, 16, 128))
VMEM_LIMIT = 40 * 2**20
MESH = pl.DeviceIdType.MESH


def rotate(values, positions):
    half = values.shape[-1] // 2
    freq = THETA ** (-(jnp.arange(half, dtype=jnp.float32) * 2.0) / values.shape[-1])
    angle = positions.astype(jnp.float32)[:, None, None] * freq[None, None, :]
    cosine = jnp.cos(angle)
    sine = jnp.sin(angle)
    first = values[..., :half]
    second = values[..., half:]
    return jnp.concatenate(
        [first * cosine - second * sine, second * cosine + first * sine], axis=-1
    )


def normalize(rows, norm_gain):
    wide = rows.astype(jnp.float32)
    scaled = wide * lax.rsqrt(jnp.mean(wide * wide, axis=-1, keepdims=True) + EPS) * norm_gain
    return scaled.astype(jnp.bfloat16)


def finish(proj, positions, key_gain, kv_heads, head_size):
    shaped = proj.reshape(proj.shape[0], kv_heads, 2, head_size)
    raw_keys = shaped[:, :, 0]
    raw_keys = (
        raw_keys * lax.rsqrt(jnp.mean(raw_keys * raw_keys, axis=-1, keepdims=True) + EPS) * key_gain
    )
    keys = rotate(raw_keys, positions).astype(jnp.bfloat16)
    values = shaped[:, :, 1].astype(jnp.bfloat16)
    return jnp.stack([keys, values], axis=2).reshape(proj.shape[0], kv_heads * 2 * head_size)


def spread(hidden, block_owner, norm_gain, kv_weight, key_gain, queries, query_pos):
    n_ctx = lax.axis_size("ctx")
    n_hst = lax.axis_size("hst")
    n_head = lax.axis_size("head")
    src_dev, rows_blk, width = hidden.shape
    head_size = key_gain.shape[0]
    kv_dev = kv_weight.shape[1] // (2 * head_size)
    kv_all = kv_dev * n_hst
    q_dev = queries.shape[1] // head_size
    group = q_dev * n_hst * n_head // kv_all
    used = max(1, q_dev // group)
    q_rows = queries.shape[0]
    ctx_i = lax.axis_index("ctx")
    hst_i = lax.axis_index("hst")
    core_i = lax.axis_index("head")
    owner = block_owner[:, 0]
    n_blk = owner.shape[0]
    code = owner * n_blk + jnp.arange(n_blk, dtype=jnp.int32)
    starts = jnp.sum((code[None, :] < code[:, None]).astype(jnp.int32), axis=1) * rows_blk
    key_pos = (starts[:, None] + jnp.arange(rows_blk, dtype=jnp.int32)[None, :]).reshape(
        n_ctx, n_hst, n_head, src_dev * rows_blk
    )
    normed = normalize(hidden.reshape(src_dev * rows_blk, width), norm_gain)
    gathered = lax.all_gather(normed, "hst", axis=0, tiled=True)
    proj = jnp.dot(gathered, kv_weight, preferred_element_type=jnp.float32)
    my_pos = lax.dynamic_index_in_dim(
        lax.dynamic_index_in_dim(key_pos, ctx_i, 0, keepdims=False), core_i, 1, keepdims=False
    ).reshape(-1)
    restored = finish(proj, my_pos, key_gain, kv_dev, head_size)
    rows = restored.shape[0]
    by_head = restored.reshape(rows, kv_dev, 2 * head_size)
    parts = [
        lax.dynamic_slice_in_dim(
            by_head, (hst_i * n_head + c) * q_dev // group - hst_i * kv_dev, used, 1
        )
        for c in range(n_head)
    ]
    mine = lax.all_to_all(jnp.stack(parts), "head", split_axis=0, concat_axis=0, tiled=True)
    full = lax.all_gather(mine.reshape(n_head * rows, used * 2 * head_size), "ctx", axis=0, tiled=True)
    full = full.reshape(-1, used, 2, head_size)
    k_pos = jnp.transpose(key_pos, (0, 2, 1, 3)).reshape(-1)
    rotated = rotate(
        queries.astype(jnp.float32).reshape(q_rows, q_dev, head_size), query_pos
    ).astype(jnp.bfloat16)
    rotated = rotated.reshape(q_rows, used, q_dev // used, head_size)
    scores = jnp.einsum(
        "qagd,kad->agqk", rotated, full[:, :, 0], preferred_element_type=jnp.float32
    ) * (1.0 / math.sqrt(head_size))
    allowed = (k_pos[None, :] <= query_pos[:, None])[None, None]
    kept = jnp.where(allowed, scores, -1e30)
    best = jnp.max(kept, axis=-1, keepdims=True)
    weights = jnp.where(allowed, jnp.exp(kept - best), 0.0)
    total = jnp.sum(weights, axis=-1, keepdims=True)
    mixed = jnp.einsum(
        "agqk,kad->agqd", weights.astype(jnp.bfloat16), full[:, :, 1], preferred_element_type=jnp.float32
    )
    result = mixed / total
    return (
        jnp.transpose(result, (2, 0, 1, 3)).reshape(q_rows, q_dev * head_size).astype(jnp.bfloat16)
    )


def log2_of(value):
    return value.bit_length() - 1


def fused(
    dims, hid_ref, own_hbm, gain_hbm, w_ref, kgain_hbm, q_hbm, qpos_hbm, freq_hbm, out_ref,
    own_ref, gain_ref, kgain_ref, q_ref, qpos_ref, freq_ref, w_v, own_rows, peer_rows, kv_send, kv_buf, q_rot, q_turn, qpos_s, kpos_s, cos_s, sin_s,
    best, total, acc, w_sem, own_sem, small_sem, hid_send, hid_recv, send_sem, recv_sem, plane_sem,
    moved_rows, moved_peer, moved_kv, moved_cos, moved_sin, moved_sem, moved_kv_send,
):
    n_ctx, n_hst, n_head, src_dev, rows_blk, chunks = dims
    rows, width = own_rows.shape
    head_size = kgain_ref.shape[1]
    half = head_size // 2
    n_blk = own_ref.shape[1]
    n_src = n_ctx * n_head
    n_chunk = len(chunks)
    firsts = [sum(chunks[:j]) for j in range(n_chunk)]
    q_rows = q_ref.shape[0]
    q_dev = q_ref.shape[1] // head_size
    z = lax.axis_index("ctx")
    x = lax.axis_index("hst")
    c = lax.axis_index("head")
    me = z * n_head + c
    peer = 1 - x
    f32 = jnp.float32
    giver_slot = (n_ctx - 1) * n_head
    giver = me == giver_slot
    keeper = me != giver_slot
    taker = me == n_head - 1
    late = n_chunk - 1
    late0, late_rows = firsts[late - 1], chunks[late - 1]
    last0, last_rows = firsts[-1], chunks[-1]

    barrier = pltpu.get_barrier_semaphore()

    pl.semaphore_signal(barrier, inc=1, device_id={"hst": peer}, device_id_type=MESH)
    head_of_plane = (n_ctx - 1) * n_head

    @pl.when(me != head_of_plane)
    def _():
        pl.semaphore_signal(
            barrier, inc=1, device_id={"ctx": n_ctx - 1, "head": 0}, device_id_type=MESH
        )

    order = []
    for k in range(n_ctx - 1):
        up = k + (k >= z).astype(jnp.int32)
        down = n_ctx - 1 - k - (n_ctx - 1 - k <= z).astype(jnp.int32)
        stop = jnp.where(2 * z >= n_ctx, up, down)
        order.append((stop, lax.rem(stop - z + n_ctx, n_ctx)))
    targets = []
    for stop, dz in order:
        for core in range(n_head):
            targets.append(({"ctx": stop, "head": core}, core, (dz - 1) * n_head + c))
    for dc in range(1, n_head):
        core = lax.rem(c + dc, n_head)
        targets.append(({"head": core}, core, (n_ctx - 1) * n_head))

    own_copy = pltpu.make_async_copy(hid_ref, own_rows, own_sem)
    own_copy.start()
    small = [
        pltpu.make_async_copy(src, dst, small_sem.at[i])
        for i, (src, dst) in enumerate(
            [
                (own_hbm, own_ref),
                (freq_hbm, freq_ref),
                (gain_hbm, gain_ref),
                (kgain_hbm, kgain_ref),
                (qpos_hbm, qpos_ref),
                (q_hbm, q_ref),
            ]
        )
    ]
    small[2].start()

    def hidden_copy(j, part=None):
        rows_j = pl.ds(firsts[j], chunks[j])
        if j == 0:
            src, dst, sem = hid_ref.at[rows_j], peer_rows.at[rows_j], 0
        elif part is None:
            src, dst, sem = own_rows.at[rows_j], peer_rows.at[rows_j], j
        else:
            columns = pl.ds(part * (width // SLICES), width // SLICES)
            src, dst, sem = own_rows.at[rows_j, columns], peer_rows.at[rows_j, columns], j + part
        return pltpu.make_async_remote_copy(
            src_ref=src,
            dst_ref=dst,
            send_sem=hid_send.at[sem],
            recv_sem=hid_recv.at[sem],
            device_id={"hst": peer},
            device_id_type=MESH,
        )

    hidden_copies = [hidden_copy(j) for j in range(n_chunk - 1)]
    last_copies = [hidden_copy(n_chunk - 1, part) for part in range(SLICES)]
    move = pltpu.make_async_remote_copy(
        src_ref=own_rows.at[pl.ds(late0, late_rows)],
        dst_ref=moved_rows,
        send_sem=moved_sem.at[0],
        recv_sem=moved_sem.at[1],
        device_id={"ctx": 0, "head": n_head - 1},
        device_id_type=MESH,
    )
    cross = pltpu.make_async_remote_copy(
        src_ref=moved_rows,
        dst_ref=moved_peer,
        send_sem=moved_sem.at[2],
        recv_sem=moved_sem.at[3],
        device_id={"hst": peer},
        device_id_type=MESH,
    )

    @pl.when(me != head_of_plane)
    def _():
        pl.semaphore_wait(barrier, 1)

    @pl.when(me == head_of_plane)
    def _():
        pl.semaphore_wait(barrier, n_src)

    hidden_copies[0].start()

    @pl.when(me == head_of_plane)
    def _():
        for stop in range(n_ctx):
            for core in range(n_head):
                if stop * n_head + core != head_of_plane:
                    device = {"ctx": stop, "head": core}
                    pl.semaphore_signal(plane_sem, inc=1, device_id=device, device_id_type=MESH)

    def plane_ready():
        @pl.when(me != head_of_plane)
        def _():
            pl.semaphore_wait(plane_sem, 1)

    w_copy = pltpu.make_async_copy(w_ref, w_v, w_sem)
    for i in (0, 1, 3):
        small[i].start()
    w_copy.start()
    for i in (4, 5):
        small[i].start()

    def normed(raw):
        wide = raw.astype(f32)
        mean = jnp.mean(wide * wide, axis=-1, keepdims=True)
        return (wide * lax.rsqrt(mean + EPS) * gain_ref[...]).astype(jnp.bfloat16)

    small[2].wait()
    own_copy.wait()
    for j in range(1, n_chunk):
        part = slice(firsts[j], firsts[j] + chunks[j])
        own_rows[part] = normed(own_rows[part])
        if j < late - 1:
            hidden_copies[j].start()
        elif j == late - 1:
            pl.when(keeper)(hidden_copies[j].start)
            pl.when(giver)(move.start)

    @pl.when(jnp.logical_not(taker))
    def _():
        for copy in last_copies:
            copy.start()

    own_rows[0 : chunks[0]] = normed(own_rows[0 : chunks[0]])

    lane = lax.broadcasted_iota(jnp.int32, (n_blk, n_blk), 1)
    sub = lax.broadcasted_iota(jnp.int32, (n_blk, n_blk), 0)
    for copy in small[:2]:
        copy.wait()
    code_row = (own_ref[...] * n_blk + lane[0:1]).astype(f32)
    code_col = jnp.sum(jnp.where(sub == lane, code_row, 0.0), axis=1, keepdims=True)
    start_col = jnp.sum(jnp.where(code_row < code_col, float(rows_blk), 0.0), axis=1, keepdims=True)
    start_row = jnp.sum(jnp.where(code_col < code_row, float(rows_blk), 0.0), axis=0, keepdims=True)

    blk_bits = log2_of(rows_blk)
    freq = freq_ref[...]
    def turns(base, row0, count):
        r = row0 + lax.broadcasted_iota(jnp.int32, (count, n_blk), 0)
        hit = lax.broadcasted_iota(jnp.int32, (count, n_blk), 1) == base + (r >> blk_bits)
        pos = jnp.sum(jnp.where(hit, start_row, 0.0), axis=1, keepdims=True)
        angle = (pos + (r[:, 0:1] & (rows_blk - 1)).astype(f32)) * freq
        low = lax.broadcasted_iota(jnp.int32, angle.shape, 1) < half
        sine = jnp.sin(angle)
        return jnp.cos(angle), jnp.where(low, -sine, sine)

    def place(side):
        source = x if side == 0 else peer
        base = ((z * n_hst + source) * n_head + c) * src_dev
        cosine, sine = turns(base, 0, rows)
        cos_s[side * rows : (side + 1) * rows] = cosine
        sin_s[side * rows : (side + 1) * rows] = sine

    place(0)

    def turned(u, cosine, sine):
        return u * cosine + pltpu.roll(u, half, 1) * sine

    def kv_copy(row0, count, sem_row, device, core, slot, sem_col):
        return pltpu.make_async_remote_copy(
            src_ref=kv_send.at[core, pl.ds(row0, count)],
            dst_ref=kv_buf.at[slot, pl.ds(row0, count)],
            send_sem=send_sem.at[sem_row, sem_col],
            recv_sem=recv_sem.at[sem_row, sem_col],
            device_id=device,
            device_id_type=MESH,
        )

    def keys_values(proj, cosine, sine):
        pairs = []
        for head in range(n_head):
            at = head * 2 * head_size
            raw = proj[:, at : at + head_size]
            scale = lax.rsqrt(jnp.mean(raw * raw, axis=-1, keepdims=True) + EPS)
            keys = turned(raw * scale * kgain_ref[...], cosine, sine).astype(jnp.bfloat16)
            values = proj[:, at + head_size : at + 2 * head_size].astype(jnp.bfloat16)
            pairs.append(jnp.concatenate([keys, values], axis=1))
        return pairs

    def finish(proj, row0, count, stage):
        pairs = keys_values(proj, cos_s[row0 : row0 + count], sin_s[row0 : row0 + count])
        kept = pairs[0]
        for head, both in enumerate(pairs):
            kv_send[head, row0 : row0 + count] = both
            kept = jnp.where(c == head, both, kept)
        kv_buf[me, row0 : row0 + count] = kept
        if stage == 0:
            plane_ready()
        for device, core, sem_col in targets:
            kv_copy(row0, count, stage, device, core, me, sem_col).start()

    moved_kv_copies = []
    for stop in range(n_ctx - 1, -1, -1):
        for core in range(n_head if stop else n_head - 1):
            sem_col = stop * n_head if stop < n_ctx - 1 else giver_slot + n_head - 1 - core
            moved_kv_copies.append(
                pltpu.make_async_remote_copy(
                    src_ref=moved_kv.at[core],
                    dst_ref=kv_buf.at[giver_slot, pl.ds(rows + late0, late_rows)],
                    send_sem=moved_kv_send.at[len(moved_kv_copies)],
                    recv_sem=recv_sem.at[late, sem_col],
                    device_id={"ctx": stop, "head": core},
                    device_id_type=MESH,
                )
            )

    def finish_moved(proj):
        pairs = keys_values(proj, moved_cos[...], moved_sin[...])
        for head, both in enumerate(pairs):
            moved_kv[head] = both
        kv_buf[giver_slot, rows + late0 : rows + late0 + late_rows] = pairs[n_head - 1]
        for copy in moved_kv_copies:
            copy.start()

    def project(rows_in, first=0, depth=None):
        depth = width if depth is None else depth
        return jnp.dot(rows_in, w_v[first : first + depth], preferred_element_type=f32)

    small[3].wait()
    w_copy.wait()
    finish(project(own_rows[...]), 0, rows, 0)
    place(1)

    @pl.when(taker)
    def _():
        base = ((n_ctx - 1) * n_hst + peer) * n_head * src_dev
        cosine, sine = turns(base, late0, late_rows)
        moved_cos[...] = cosine
        moved_sin[...] = sine


    r = lax.broadcasted_iota(jnp.int32, (rows, n_blk), 0)
    for side in range(2):
        source = x if side == 0 else peer
        for s in range(n_src):
            base = (((s // n_head) * n_hst + source) * n_head + s % n_head) * src_dev
            hit = lax.broadcasted_iota(jnp.int32, (rows, n_blk), 1) == base + (r >> blk_bits)
            pos = jnp.sum(jnp.where(hit, start_row, 0.0), axis=1, keepdims=True)
            pos = pos + (r[:, 0:1] & (rows_blk - 1)).astype(f32)
            for _, row0, count, _, _ in PLAN:
                if row0 // rows == side:
                    first = n_src * row0 + s * count
                    kpos_s[first : first + count] = pos[row0 % rows : row0 % rows + count]

    for copy in small[4:]:
        copy.wait()
    row = lax.broadcasted_iota(jnp.int32, (q_rows, q_rows), 0)
    column = lax.broadcasted_iota(jnp.int32, (q_rows, q_rows), 1)
    qpos = jnp.where(row == column, qpos_ref[...].astype(f32), 0.0)
    qpos = jnp.sum(qpos, axis=1, keepdims=True)
    q_angle = qpos * freq
    q_sine = jnp.sin(q_angle)
    low = lax.broadcasted_iota(jnp.int32, q_angle.shape, 1) < half
    q_sine = jnp.where(low, -q_sine, q_sine)
    q_cosine = jnp.cos(q_angle)
    for head in range(q_dev):
        u = q_ref[:, head * head_size : (head + 1) * head_size].astype(f32)
        q_rot[head * q_rows : (head + 1) * q_rows] = turned(u, q_cosine, q_sine)
    q_turn[...] = q_rot[...].T.astype(jnp.bfloat16)
    qpos_row = qpos_ref[...].astype(f32)
    qpos_s[...] = jnp.concatenate([qpos_row] * q_dev, axis=1)
    best[...] = jnp.full_like(best, -1e30)
    total[...] = jnp.zeros_like(total)
    acc[...] = jnp.zeros_like(acc)
    factor = math.log2(math.e) / math.sqrt(head_size)

    def put(mix, denom):
        result = (mix * (1.0 / denom)).T
        for head in range(q_dev):
            out_ref[:, head * head_size : (head + 1) * head_size] = result[
                head * q_rows : (head + 1) * q_rows
            ].astype(out_ref.dtype)

    def attend(row0, count, tiles, step, last):
        at = n_src * row0
        span = n_src * count
        tile = tiles * q_rows
        step = min(step, span)
        keys = kv_buf[:, row0 : row0 + count, 0:head_size].reshape(span, head_size)
        values = kv_buf[:, row0 : row0 + count, head_size : 2 * head_size].reshape(span, head_size)

        def block(i, carry):
            part = slice(None) if last else pl.ds(pl.multiple_of(i * tile, tile), tile)
            q_part = q_turn[:, part]
            qpos_part = qpos_s[:, part]
            top, denom, mix = best[:, part], total[:, part], acc[:, part]
            for first in range(0, span, step):
                scores = jnp.dot(keys[first : first + step], q_part, preferred_element_type=f32)
                kpos = kpos_s[at + first : at + first + step]
                kept = jnp.where(kpos <= qpos_part, scores, -2e30)
                new = jnp.maximum(top, jnp.max(kept, axis=0, keepdims=True))
                weights = jnp.exp2((kept - new) * factor)
                fade = jnp.exp2((top - new) * factor)
                top = new
                denom = denom * fade + jnp.sum(weights, axis=0, keepdims=True)
                mix = mix * fade + lax.dot_general(
                    values[first : first + step],
                    weights.astype(jnp.bfloat16),
                    (((0,), (0,)), ((), ())),
                    preferred_element_type=f32,
                )
            if last:
                put(mix, denom)
                return carry
            best[:, part] = top
            total[:, part] = denom
            acc[:, part] = mix
            return carry

        if last:
            block(0, 0)
        else:
            lax.fori_loop(0, q_dev * q_rows // tile, block, 0)

    def arrive(row0, count, stage):
        def one(slot, sem_col):
            kv_copy(row0, count, stage, targets[0][0], 0, slot, sem_col).wait_recv()

        for dz in range(1, n_ctx):
            for core in range(n_head):
                slot = lax.rem(z + n_ctx - dz, n_ctx) * n_head + core
                wait = functools.partial(one, slot, (dz - 1) * n_head + core)
                if stage == late and dz == 1 and core == 0:
                    pl.when(jnp.logical_not(taker))(wait)
                else:
                    wait()
        for dc in range(1, n_head):
            one(z * n_head + lax.rem(c + n_head - dc, n_head), giver_slot)
        if stage == late:
            pl.when(giver)(functools.partial(one, giver_slot, giver_slot + 1))

    def sliced(copies, rows_ref, row0, count):
        proj = None
        depth = width // SLICES
        for i, copy in enumerate(copies):
            copy.wait_recv()
            term = project(rows_ref[row0 : row0 + count, i * depth : (i + 1) * depth], i * depth, depth)
            proj = term if proj is None else proj + term
        return proj

    @pl.when(taker)
    def _():
        move.wait_recv()
        cross.start()
        for copy in last_copies:
            copy.start()

    spans = [(0, rows)] + [(rows + firsts[j], chunks[j]) for j in range(n_chunk)]
    for stage in range(1, n_chunk + 1):

        def restore(stage=stage):
            hidden_copies[stage - 1].wait_recv()
            arrived = peer_rows[firsts[stage - 1] : firsts[stage - 1] + chunks[stage - 1]]
            finish(project(normed(arrived) if stage == 1 else arrived), *spans[stage], stage)

        if stage == n_chunk:
            finish(sliced(last_copies, peer_rows, last0, last_rows), *spans[stage], stage)
        elif stage == late:
            pl.when(keeper)(restore)

            @pl.when(taker)
            def _():
                cross.wait_recv()
                finish_moved(project(moved_peer[...]))
        else:
            restore()

        for i_plan, (after, row0, count, tiles, step) in enumerate(PLAN):
            if after == stage:
                for i, (first, size) in enumerate(spans):
                    if row0 <= first < row0 + count:
                        arrive(first, size, i)
                attend(row0, count, tiles, step, i_plan == len(PLAN) - 1)

    def sent(stage):
        for device, core, sem_col in targets:
            kv_copy(*spans[stage], stage, device, core, me, sem_col).wait_send()

    def sent(stage):
        for device, core, sem_col in targets:
            kv_copy(*spans[stage], stage, device, core, me, sem_col).wait_send()

    for j, copy in enumerate(hidden_copies):
        if j != late - 1:
            copy.wait_send()
    for copy in last_copies:
        copy.wait_send()
    for stage in range(n_chunk + 1):
        if stage != late:
            sent(stage)

    @pl.when(keeper)
    def _():
        hidden_copies[late - 1].wait_send()
        sent(late)

    @pl.when(giver)
    def _():
        move.wait_send()

    @pl.when(taker)
    def _():
        for copy in [cross] + moved_kv_copies:
            copy.wait_send()


def body(hidden, block_owner, norm_gain, kv_weight, key_gain, queries, query_pos):
    n_ctx = lax.axis_size("ctx")
    n_hst = lax.axis_size("hst")
    n_head = lax.axis_size("head")
    src_dev, rows_blk, width = hidden.shape
    head_size = key_gain.shape[0]
    kv_dev = kv_weight.shape[1] // (2 * head_size)
    q_rows = queries.shape[0]
    q_dev = queries.shape[1] // head_size
    if n_hst != 2 or n_head != 2 or kv_dev != n_head or n_ctx not in (2, 4) or src_dev * rows_blk != sum(CHUNKS):
        return spread(hidden, block_owner, norm_gain, kv_weight, key_gain, queries, query_pos)
    rows = src_dev * rows_blk
    n_chunk = len(CHUNKS)
    n_src = n_ctx * n_head
    n_peer = n_src - 1
    half = head_size // 2
    freq = THETA ** (-(np.arange(half, dtype=np.float64) * 2.0) / head_size)
    freq = jnp.asarray(np.concatenate([freq, freq]).astype(np.float32)[None])
    vmem = pl.BlockSpec(memory_space=pltpu.VMEM)
    hbm = pl.BlockSpec(memory_space=pltpu.HBM)
    bf16, f32 = jnp.bfloat16, jnp.float32
    return pl.pallas_call(
        functools.partial(fused, (n_ctx, n_hst, n_head, src_dev, rows_blk, CHUNKS)),
        out_shape=jax.ShapeDtypeStruct(queries.shape, bf16),
        in_specs=[hbm] * 8,
        out_specs=vmem,
        scratch_shapes=[
            pltpu.VMEM((1, block_owner.shape[0]), jnp.int32),
            pltpu.VMEM((1, width), f32),
            pltpu.VMEM((1, head_size), f32),
            pltpu.VMEM(queries.shape, bf16),
            pltpu.VMEM((1, q_rows), jnp.int32),
            pltpu.VMEM((1, head_size), f32),
            pltpu.VMEM(kv_weight.shape, bf16),
            pltpu.VMEM((rows, width), bf16),
            pltpu.VMEM((rows, width), bf16),
            pltpu.VMEM((n_head, 2 * rows, 2 * head_size), bf16),
            pltpu.VMEM((n_src, 2 * rows, 2 * head_size), bf16),
            pltpu.VMEM((q_dev * q_rows, head_size), f32),
            pltpu.VMEM((head_size, q_dev * q_rows), bf16),
            pltpu.VMEM((1, q_dev * q_rows), f32),
            pltpu.VMEM((n_src * 2 * rows, 1), f32),
            pltpu.VMEM((2 * rows, head_size), f32),
            pltpu.VMEM((2 * rows, head_size), f32),
            pltpu.VMEM((1, q_dev * q_rows), f32),
            pltpu.VMEM((1, q_dev * q_rows), f32),
            pltpu.VMEM((head_size, q_dev * q_rows), f32),
            pltpu.SemaphoreType.DMA,
            pltpu.SemaphoreType.DMA,
            pltpu.SemaphoreType.DMA((6,)),
            pltpu.SemaphoreType.DMA((n_chunk - 1 + SLICES,)),
            pltpu.SemaphoreType.DMA((n_chunk - 1 + SLICES,)),
            pltpu.SemaphoreType.DMA((n_chunk + 1, n_peer)),
            pltpu.SemaphoreType.DMA((n_chunk + 1, n_peer + 1)),
            pltpu.SemaphoreType.REGULAR,
            pltpu.VMEM((CHUNKS[-2], width), bf16),
            pltpu.VMEM((CHUNKS[-2], width), bf16),
            pltpu.VMEM((n_head, CHUNKS[-2], 2 * head_size), bf16),
            pltpu.VMEM((CHUNKS[-2], head_size), f32),
            pltpu.VMEM((CHUNKS[-2], head_size), f32),
            pltpu.SemaphoreType.DMA((4,)),
            pltpu.SemaphoreType.DMA((n_peer,)),
        ],
        compiler_params=pltpu.CompilerParams(
            collective_id=0, has_side_effects=True, vmem_limit_bytes=VMEM_LIMIT
        ),
    )(
        *[
            pltpu.with_memory_space_constraint(array, pltpu.HBM)
            for array in (
                hidden.reshape(rows, width),
                block_owner.reshape(1, -1),
                norm_gain[None],
                kv_weight,
                key_gain[None],
                queries,
                query_pos[None],
                freq,
            )
        ]
    )


def solution(mesh):
    in_specs = (
        P(("groups", "ctx", "hst", "head"), None, None),
        P("groups", None),
        P(),
        P(None, "hst"),
        P(),
        P(("groups", "ctx"), ("hst", "head")),
        P(("groups", "ctx")),
    )
    out_specs = P(("groups", "ctx"), ("hst", "head"))
    return jax.shard_map(body, mesh=mesh, in_specs=in_specs, out_specs=out_specs, check_vma=False)
```

```python
import functools
import math

import jax
import jax.numpy as jnp
import numpy as np
from jax import lax
from jax.experimental import pallas as pl
from jax.experimental.pallas import tpu as pltpu
from jax.sharding import PartitionSpec as P

EPS = 1e-06
THETA = 1000000.0
CHUNKS = (64, 32, 16, 16)
SLICES = 2
PLAN = ((2, 0, 128, 8, 1024), (4, 128, 64, 8, 512), (4, 192, 32, 16, 256), (4, 224, 16, 16, 128), (4, 240, 16, 16, 128))
VMEM_LIMIT = 40 * 2**20
MESH = pl.DeviceIdType.MESH


def rotate(values, positions):
    half = values.shape[-1] // 2
    freq = THETA ** (-(jnp.arange(half, dtype=jnp.float32) * 2.0) / values.shape[-1])
    angle = positions.astype(jnp.float32)[:, None, None] * freq[None, None, :]
    cosine = jnp.cos(angle)
    sine = jnp.sin(angle)
    first = values[..., :half]
    second = values[..., half:]
    return jnp.concatenate(
        [first * cosine - second * sine, second * cosine + first * sine], axis=-1
    )


def normalize(rows, norm_gain):
    wide = rows.astype(jnp.float32)
    scaled = wide * lax.rsqrt(jnp.mean(wide * wide, axis=-1, keepdims=True) + EPS) * norm_gain
    return scaled.astype(jnp.bfloat16)


def finish(proj, positions, key_gain, kv_heads, head_size):
    shaped = proj.reshape(proj.shape[0], kv_heads, 2, head_size)
    raw_keys = shaped[:, :, 0]
    raw_keys = (
        raw_keys * lax.rsqrt(jnp.mean(raw_keys * raw_keys, axis=-1, keepdims=True) + EPS) * key_gain
    )
    keys = rotate(raw_keys, positions).astype(jnp.bfloat16)
    values = shaped[:, :, 1].astype(jnp.bfloat16)
    return jnp.stack([keys, values], axis=2).reshape(proj.shape[0], kv_heads * 2 * head_size)


def spread(hidden, block_owner, norm_gain, kv_weight, key_gain, queries, query_pos):
    n_ctx = lax.axis_size("ctx")
    n_hst = lax.axis_size("hst")
    n_head = lax.axis_size("head")
    src_dev, rows_blk, width = hidden.shape
    head_size = key_gain.shape[0]
    kv_dev = kv_weight.shape[1] // (2 * head_size)
    kv_all = kv_dev * n_hst
    q_dev = queries.shape[1] // head_size
    group = q_dev * n_hst * n_head // kv_all
    used = max(1, q_dev // group)
    q_rows = queries.shape[0]
    ctx_i = lax.axis_index("ctx")
    hst_i = lax.axis_index("hst")
    core_i = lax.axis_index("head")
    owner = block_owner[:, 0]
    n_blk = owner.shape[0]
    code = owner * n_blk + jnp.arange(n_blk, dtype=jnp.int32)
    starts = jnp.sum((code[None, :] < code[:, None]).astype(jnp.int32), axis=1) * rows_blk
    key_pos = (starts[:, None] + jnp.arange(rows_blk, dtype=jnp.int32)[None, :]).reshape(
        n_ctx, n_hst, n_head, src_dev * rows_blk
    )
    normed = normalize(hidden.reshape(src_dev * rows_blk, width), norm_gain)
    gathered = lax.all_gather(normed, "hst", axis=0, tiled=True)
    proj = jnp.dot(gathered, kv_weight, preferred_element_type=jnp.float32)
    my_pos = lax.dynamic_index_in_dim(
        lax.dynamic_index_in_dim(key_pos, ctx_i, 0, keepdims=False), core_i, 1, keepdims=False
    ).reshape(-1)
    restored = finish(proj, my_pos, key_gain, kv_dev, head_size)
    rows = restored.shape[0]
    by_head = restored.reshape(rows, kv_dev, 2 * head_size)
    parts = [
        lax.dynamic_slice_in_dim(
            by_head, (hst_i * n_head + c) * q_dev // group - hst_i * kv_dev, used, 1
        )
        for c in range(n_head)
    ]
    mine = lax.all_to_all(jnp.stack(parts), "head", split_axis=0, concat_axis=0, tiled=True)
    full = lax.all_gather(mine.reshape(n_head * rows, used * 2 * head_size), "ctx", axis=0, tiled=True)
    full = full.reshape(-1, used, 2, head_size)
    k_pos = jnp.transpose(key_pos, (0, 2, 1, 3)).reshape(-1)
    rotated = rotate(
        queries.astype(jnp.float32).reshape(q_rows, q_dev, head_size), query_pos
    ).astype(jnp.bfloat16)
    rotated = rotated.reshape(q_rows, used, q_dev // used, head_size)
    scores = jnp.einsum(
        "qagd,kad->agqk", rotated, full[:, :, 0], preferred_element_type=jnp.float32
    ) * (1.0 / math.sqrt(head_size))
    allowed = (k_pos[None, :] <= query_pos[:, None])[None, None]
    kept = jnp.where(allowed, scores, -1e30)
    best = jnp.max(kept, axis=-1, keepdims=True)
    weights = jnp.where(allowed, jnp.exp(kept - best), 0.0)
    total = jnp.sum(weights, axis=-1, keepdims=True)
    mixed = jnp.einsum(
        "agqk,kad->agqd", weights.astype(jnp.bfloat16), full[:, :, 1], preferred_element_type=jnp.float32
    )
    result = mixed / total
    return (
        jnp.transpose(result, (2, 0, 1, 3)).reshape(q_rows, q_dev * head_size).astype(jnp.bfloat16)
    )


def log2_of(value):
    return value.bit_length() - 1


def fused(
    dims, hid_ref, own_hbm, gain_hbm, w_ref, kgain_hbm, q_hbm, qpos_hbm, freq_hbm, out_ref,
    own_ref, gain_ref, kgain_ref, q_ref, qpos_ref, freq_ref, w_v, own_rows, peer_rows, kv_send, kv_buf, q_rot, q_turn, qpos_s, kpos_s, cos_s, sin_s,
    best, total, acc, w_sem, own_sem, small_sem, hid_send, hid_recv, send_sem, recv_sem, plane_sem,
    moved_rows, moved_peer, moved_kv, moved_cos, moved_sin, moved_sem, moved_kv_send,
):
    n_ctx, n_hst, n_head, src_dev, rows_blk, chunks = dims
    rows, width = own_rows.shape
    head_size = kgain_ref.shape[1]
    half = head_size // 2
    n_blk = own_ref.shape[1]
    n_src = n_ctx * n_head
    n_chunk = len(chunks)
    firsts = [sum(chunks[:j]) for j in range(n_chunk)]
    q_rows = q_ref.shape[0]
    q_dev = q_ref.shape[1] // head_size
    z = lax.axis_index("ctx")
    x = lax.axis_index("hst")
    c = lax.axis_index("head")
    me = z * n_head + c
    peer = 1 - x
    f32 = jnp.float32
    giver_slot = (n_ctx - 1) * n_head
    giver = me == giver_slot
    keeper = me != giver_slot
    taker = me == n_head - 1
    late = n_chunk - 1
    late0, late_rows = firsts[late - 1], chunks[late - 1]
    last0, last_rows = firsts[-1], chunks[-1]

    barrier = pltpu.get_barrier_semaphore()

    pl.semaphore_signal(barrier, inc=1, device_id={"hst": peer}, device_id_type=MESH)
    head_of_plane = (n_ctx - 1) * n_head

    @pl.when(me != head_of_plane)
    def _():
        pl.semaphore_signal(
            barrier, inc=1, device_id={"ctx": n_ctx - 1, "head": 0}, device_id_type=MESH
        )

    order = []
    for k in range(n_ctx - 1):
        up = k + (k >= z).astype(jnp.int32)
        down = n_ctx - 1 - k - (n_ctx - 1 - k <= z).astype(jnp.int32)
        stop = jnp.where(2 * z >= n_ctx, up, down)
        order.append((stop, lax.rem(stop - z + n_ctx, n_ctx)))
    targets = []
    for stop, dz in order:
        for core in range(n_head):
            targets.append(({"ctx": stop, "head": core}, core, (dz - 1) * n_head + c))
    for dc in range(1, n_head):
        core = lax.rem(c + dc, n_head)
        targets.append(({"head": core}, core, (n_ctx - 1) * n_head))

    own_copy = pltpu.make_async_copy(hid_ref, own_rows, own_sem)
    own_copy.start()
    small = [
        pltpu.make_async_copy(src, dst, small_sem.at[i])
        for i, (src, dst) in enumerate(
            [
                (own_hbm, own_ref),
                (freq_hbm, freq_ref),
                (gain_hbm, gain_ref),
                (kgain_hbm, kgain_ref),
                (qpos_hbm, qpos_ref),
                (q_hbm, q_ref),
            ]
        )
    ]
    small[2].start()

    def hidden_copy(j, part=None):
        rows_j = pl.ds(firsts[j], chunks[j])
        if j == 0:
            src, dst, sem = hid_ref.at[rows_j], peer_rows.at[rows_j], 0
        elif part is None:
            src, dst, sem = own_rows.at[rows_j], peer_rows.at[rows_j], j
        else:
            columns = pl.ds(part * (width // SLICES), width // SLICES)
            src, dst, sem = own_rows.at[rows_j, columns], peer_rows.at[rows_j, columns], j + part
        return pltpu.make_async_remote_copy(
            src_ref=src,
            dst_ref=dst,
            send_sem=hid_send.at[sem],
            recv_sem=hid_recv.at[sem],
            device_id={"hst": peer},
            device_id_type=MESH,
        )

    hidden_copies = [hidden_copy(j) for j in range(n_chunk - 1)]
    last_copies = [hidden_copy(n_chunk - 1, part) for part in range(SLICES)]
    move = pltpu.make_async_remote_copy(
        src_ref=own_rows.at[pl.ds(late0, late_rows)],
        dst_ref=moved_rows,
        send_sem=moved_sem.at[0],
        recv_sem=moved_sem.at[1],
        device_id={"ctx": 0, "head": n_head - 1},
        device_id_type=MESH,
    )
    cross = pltpu.make_async_remote_copy(
        src_ref=moved_rows,
        dst_ref=moved_peer,
        send_sem=moved_sem.at[2],
        recv_sem=moved_sem.at[3],
        device_id={"hst": peer},
        device_id_type=MESH,
    )

    @pl.when(me != head_of_plane)
    def _():
        pl.semaphore_wait(barrier, 1)

    @pl.when(me == head_of_plane)
    def _():
        pl.semaphore_wait(barrier, n_src)

    hidden_copies[0].start()

    @pl.when(me == head_of_plane)
    def _():
        for stop in range(n_ctx):
            for core in range(n_head):
                if stop * n_head + core != head_of_plane:
                    device = {"ctx": stop, "head": core}
                    pl.semaphore_signal(plane_sem, inc=1, device_id=device, device_id_type=MESH)

    def plane_ready():
        @pl.when(me != head_of_plane)
        def _():
            pl.semaphore_wait(plane_sem, 1)

    w_copy = pltpu.make_async_copy(w_ref, w_v, w_sem)
    for i in (0, 1, 3):
        small[i].start()
    w_copy.start()
    for i in (4, 5):
        small[i].start()

    def normed(raw):
        wide = raw.astype(f32)
        mean = jnp.mean(wide * wide, axis=-1, keepdims=True)
        return (wide * lax.rsqrt(mean + EPS) * gain_ref[...]).astype(jnp.bfloat16)

    small[2].wait()
    own_copy.wait()
    for j in range(1, n_chunk):
        part = slice(firsts[j], firsts[j] + chunks[j])
        own_rows[part] = normed(own_rows[part])
        if j < late - 1:
            hidden_copies[j].start()
        elif j == late - 1:
            pl.when(keeper)(hidden_copies[j].start)
            pl.when(giver)(move.start)

    @pl.when(jnp.logical_not(taker))
    def _():
        for copy in last_copies:
            copy.start()

    own_rows[0 : chunks[0]] = normed(own_rows[0 : chunks[0]])

    lane = lax.broadcasted_iota(jnp.int32, (n_blk, n_blk), 1)
    sub = lax.broadcasted_iota(jnp.int32, (n_blk, n_blk), 0)
    for copy in small[:2]:
        copy.wait()
    code_row = (own_ref[...] * n_blk + lane[0:1]).astype(f32)
    code_col = jnp.sum(jnp.where(sub == lane, code_row, 0.0), axis=1, keepdims=True)
    start_col = jnp.sum(jnp.where(code_row < code_col, float(rows_blk), 0.0), axis=1, keepdims=True)
    start_row = jnp.sum(jnp.where(code_col < code_row, float(rows_blk), 0.0), axis=0, keepdims=True)

    blk_bits = log2_of(rows_blk)
    freq = freq_ref[...]
    def turns(base, row0, count):
        r = row0 + lax.broadcasted_iota(jnp.int32, (count, n_blk), 0)
        hit = lax.broadcasted_iota(jnp.int32, (count, n_blk), 1) == base + (r >> blk_bits)
        pos = jnp.sum(jnp.where(hit, start_row, 0.0), axis=1, keepdims=True)
        angle = (pos + (r[:, 0:1] & (rows_blk - 1)).astype(f32)) * freq
        low = lax.broadcasted_iota(jnp.int32, angle.shape, 1) < half
        sine = jnp.sin(angle)
        return jnp.cos(angle), jnp.where(low, -sine, sine)

    def place(side):
        source = x if side == 0 else peer
        base = ((z * n_hst + source) * n_head + c) * src_dev
        cosine, sine = turns(base, 0, rows)
        cos_s[side * rows : (side + 1) * rows] = cosine
        sin_s[side * rows : (side + 1) * rows] = sine

    place(0)

    def turned(u, cosine, sine):
        return u * cosine + pltpu.roll(u, half, 1) * sine

    def kv_copy(row0, count, sem_row, device, core, slot, sem_col):
        return pltpu.make_async_remote_copy(
            src_ref=kv_send.at[core, pl.ds(row0, count)],
            dst_ref=kv_buf.at[slot, pl.ds(row0, count)],
            send_sem=send_sem.at[sem_row, sem_col],
            recv_sem=recv_sem.at[sem_row, sem_col],
            device_id=device,
            device_id_type=MESH,
        )

    def keys_values(proj, cosine, sine):
        pairs = []
        for head in range(n_head):
            at = head * 2 * head_size
            raw = proj[:, at : at + head_size]
            scale = lax.rsqrt(jnp.mean(raw * raw, axis=-1, keepdims=True) + EPS)
            keys = turned(raw * scale * kgain_ref[...], cosine, sine).astype(jnp.bfloat16)
            values = proj[:, at + head_size : at + 2 * head_size].astype(jnp.bfloat16)
            pairs.append(jnp.concatenate([keys, values], axis=1))
        return pairs

    def finish(proj, row0, count, stage):
        pairs = keys_values(proj, cos_s[row0 : row0 + count], sin_s[row0 : row0 + count])
        kept = pairs[0]
        for head, both in enumerate(pairs):
            kv_send[head, row0 : row0 + count] = both
            kept = jnp.where(c == head, both, kept)
        kv_buf[me, row0 : row0 + count] = kept
        if stage == 0:
            plane_ready()
        for device, core, sem_col in targets:
            kv_copy(row0, count, stage, device, core, me, sem_col).start()

    moved_kv_copies = []
    for stop in range(n_ctx - 1, -1, -1):
        for core in range(n_head if stop else n_head - 1):
            sem_col = stop * n_head if stop < n_ctx - 1 else giver_slot + n_head - 1 - core
            moved_kv_copies.append(
                pltpu.make_async_remote_copy(
                    src_ref=moved_kv.at[core],
                    dst_ref=kv_buf.at[giver_slot, pl.ds(rows + late0, late_rows)],
                    send_sem=moved_kv_send.at[len(moved_kv_copies)],
                    recv_sem=recv_sem.at[late, sem_col],
                    device_id={"ctx": stop, "head": core},
                    device_id_type=MESH,
                )
            )

    def finish_moved(proj):
        pairs = keys_values(proj, moved_cos[...], moved_sin[...])
        for head, both in enumerate(pairs):
            moved_kv[head] = both
        kv_buf[giver_slot, rows + late0 : rows + late0 + late_rows] = pairs[n_head - 1]
        for copy in moved_kv_copies:
            copy.start()

    def project(rows_in, first=0, depth=None):
        depth = width if depth is None else depth
        return jnp.dot(rows_in, w_v[first : first + depth], preferred_element_type=f32)

    small[3].wait()
    w_copy.wait()
    finish(project(own_rows[...]), 0, rows, 0)
    place(1)

    @pl.when(taker)
    def _():
        base = ((n_ctx - 1) * n_hst + peer) * n_head * src_dev
        cosine, sine = turns(base, late0, late_rows)
        moved_cos[...] = cosine
        moved_sin[...] = sine


    r = lax.broadcasted_iota(jnp.int32, (rows, n_blk), 0)
    for side in range(2):
        source = x if side == 0 else peer
        for s in range(n_src):
            base = (((s // n_head) * n_hst + source) * n_head + s % n_head) * src_dev
            hit = lax.broadcasted_iota(jnp.int32, (rows, n_blk), 1) == base + (r >> blk_bits)
            pos = jnp.sum(jnp.where(hit, start_row, 0.0), axis=1, keepdims=True)
            pos = pos + (r[:, 0:1] & (rows_blk - 1)).astype(f32)
            for _, row0, count, _, _ in PLAN:
                if row0 // rows == side:
                    first = n_src * row0 + s * count
                    kpos_s[first : first + count] = pos[row0 % rows : row0 % rows + count]

    for copy in small[4:]:
        copy.wait()
    row = lax.broadcasted_iota(jnp.int32, (q_rows, q_rows), 0)
    column = lax.broadcasted_iota(jnp.int32, (q_rows, q_rows), 1)
    qpos = jnp.where(row == column, qpos_ref[...].astype(f32), 0.0)
    qpos = jnp.sum(qpos, axis=1, keepdims=True)
    q_angle = qpos * freq
    q_sine = jnp.sin(q_angle)
    low = lax.broadcasted_iota(jnp.int32, q_angle.shape, 1) < half
    q_sine = jnp.where(low, -q_sine, q_sine)
    q_cosine = jnp.cos(q_angle)
    for head in range(q_dev):
        u = q_ref[:, head * head_size : (head + 1) * head_size].astype(f32)
        q_rot[head * q_rows : (head + 1) * q_rows] = turned(u, q_cosine, q_sine)
    q_turn[...] = q_rot[...].T.astype(jnp.bfloat16)
    qpos_row = qpos_ref[...].astype(f32)
    qpos_s[...] = jnp.concatenate([qpos_row] * q_dev, axis=1)
    best[...] = jnp.full_like(best, -1e30)
    total[...] = jnp.zeros_like(total)
    acc[...] = jnp.zeros_like(acc)
    factor = math.log2(math.e) / math.sqrt(head_size)

    def put(mix, denom):
        result = (mix * (1.0 / denom)).T
        for head in range(q_dev):
            out_ref[:, head * head_size : (head + 1) * head_size] = result[
                head * q_rows : (head + 1) * q_rows
            ].astype(out_ref.dtype)

    def attend(row0, count, tiles, step, last):
        at = n_src * row0
        span = n_src * count
        tile = tiles * q_rows
        step = min(step, span)
        keys = kv_buf[:, row0 : row0 + count, 0:head_size].reshape(span, head_size)
        values = kv_buf[:, row0 : row0 + count, head_size : 2 * head_size].reshape(span, head_size)

        def block(i, carry):
            part = slice(None) if last else pl.ds(pl.multiple_of(i * tile, tile), tile)
            q_part = q_turn[:, part]
            qpos_part = qpos_s[:, part]
            top, denom, mix = best[:, part], total[:, part], acc[:, part]
            for first in range(0, span, step):
                scores = jnp.dot(keys[first : first + step], q_part, preferred_element_type=f32)
                kpos = kpos_s[at + first : at + first + step]
                kept = jnp.where(kpos <= qpos_part, scores, -2e30)
                new = jnp.maximum(top, jnp.max(kept, axis=0, keepdims=True))
                weights = jnp.exp2((kept - new) * factor)
                fade = jnp.exp2((top - new) * factor)
                top = new
                denom = denom * fade + jnp.sum(weights, axis=0, keepdims=True)
                mix = mix * fade + lax.dot_general(
                    values[first : first + step],
                    weights.astype(jnp.bfloat16),
                    (((0,), (0,)), ((), ())),
                    preferred_element_type=f32,
                )
            if last:
                put(mix, denom)
                return carry
            best[:, part] = top
            total[:, part] = denom
            acc[:, part] = mix
            return carry

        if last:
            block(0, 0)
        else:
            lax.fori_loop(0, q_dev * q_rows // tile, block, 0)

    def arrive(row0, count, stage):
        def one(slot, sem_col):
            kv_copy(row0, count, stage, targets[0][0], 0, slot, sem_col).wait_recv()

        for dz in range(1, n_ctx):
            for core in range(n_head):
                slot = lax.rem(z + n_ctx - dz, n_ctx) * n_head + core
                wait = functools.partial(one, slot, (dz - 1) * n_head + core)
                if stage == late and dz == 1 and core == 0:
                    pl.when(jnp.logical_not(taker))(wait)
                else:
                    wait()
        for dc in range(1, n_head):
            one(z * n_head + lax.rem(c + n_head - dc, n_head), giver_slot)
        if stage == late:
            pl.when(giver)(functools.partial(one, giver_slot, giver_slot + 1))

    def sliced(copies, rows_ref, row0, count):
        proj = None
        depth = width // SLICES
        for i, copy in enumerate(copies):
            copy.wait_recv()
            term = project(rows_ref[row0 : row0 + count, i * depth : (i + 1) * depth], i * depth, depth)
            proj = term if proj is None else proj + term
        return proj

    @pl.when(taker)
    def _():
        move.wait_recv()
        cross.start()
        for copy in last_copies:
            copy.start()

    spans = [(0, rows)] + [(rows + firsts[j], chunks[j]) for j in range(n_chunk)]
    for stage in range(1, n_chunk + 1):

        def restore(stage=stage):
            hidden_copies[stage - 1].wait_recv()
            arrived = peer_rows[firsts[stage - 1] : firsts[stage - 1] + chunks[stage - 1]]
            finish(project(normed(arrived) if stage == 1 else arrived), *spans[stage], stage)

        if stage == n_chunk:
            finish(sliced(last_copies, peer_rows, last0, last_rows), *spans[stage], stage)
        elif stage == late:
            pl.when(keeper)(restore)

            @pl.when(taker)
            def _():
                cross.wait_recv()
                finish_moved(project(moved_peer[...]))
        else:
            restore()

        for i_plan, (after, row0, count, tiles, step) in enumerate(PLAN):
            if after == stage:
                for i, (first, size) in enumerate(spans):
                    if row0 <= first < row0 + count:
                        arrive(first, size, i)
                attend(row0, count, tiles, step, i_plan == len(PLAN) - 1)

    def sent(stage):
        for device, core, sem_col in targets:
            kv_copy(*spans[stage], stage, device, core, me, sem_col).wait_send()

    def sent(stage):
        for device, core, sem_col in targets:
            kv_copy(*spans[stage], stage, device, core, me, sem_col).wait_send()

    for j, copy in enumerate(hidden_copies):
        if j != late - 1:
            copy.wait_send()
    for copy in last_copies:
        copy.wait_send()
    for stage in range(n_chunk + 1):
        if stage != late:
            sent(stage)

    @pl.when(keeper)
    def _():
        hidden_copies[late - 1].wait_send()
        sent(late)

    @pl.when(giver)
    def _():
        move.wait_send()

    @pl.when(taker)
    def _():
        for copy in [cross] + moved_kv_copies:
            copy.wait_send()


def body(hidden, block_owner, norm_gain, kv_weight, key_gain, queries, query_pos):
    n_ctx = lax.axis_size("ctx")
    n_hst = lax.axis_size("hst")
    n_head = lax.axis_size("head")
    src_dev, rows_blk, width = hidden.shape
    head_size = key_gain.shape[0]
    kv_dev = kv_weight.shape[1] // (2 * head_size)
    q_rows = queries.shape[0]
    q_dev = queries.shape[1] // head_size
    if n_hst != 2 or n_head != 2 or kv_dev != n_head or n_ctx not in (2, 4) or src_dev * rows_blk != sum(CHUNKS):
        return spread(hidden, block_owner, norm_gain, kv_weight, key_gain, queries, query_pos)
    rows = src_dev * rows_blk
    n_chunk = len(CHUNKS)
    n_src = n_ctx * n_head
    n_peer = n_src - 1
    half = head_size // 2
    freq = THETA ** (-(np.arange(half, dtype=np.float64) * 2.0) / head_size)
    freq = jnp.asarray(np.concatenate([freq, freq]).astype(np.float32)[None])
    vmem = pl.BlockSpec(memory_space=pltpu.VMEM)
    hbm = pl.BlockSpec(memory_space=pltpu.HBM)
    bf16, f32 = jnp.bfloat16, jnp.float32
    return pl.pallas_call(
        functools.partial(fused, (n_ctx, n_hst, n_head, src_dev, rows_blk, CHUNKS)),
        out_shape=jax.ShapeDtypeStruct(queries.shape, bf16),
        in_specs=[hbm] * 8,
        out_specs=vmem,
        scratch_shapes=[
            pltpu.VMEM((1, block_owner.shape[0]), jnp.int32),
            pltpu.VMEM((1, width), f32),
            pltpu.VMEM((1, head_size), f32),
            pltpu.VMEM(queries.shape, bf16),
            pltpu.VMEM((1, q_rows), jnp.int32),
            pltpu.VMEM((1, head_size), f32),
            pltpu.VMEM(kv_weight.shape, bf16),
            pltpu.VMEM((rows, width), bf16),
            pltpu.VMEM((rows, width), bf16),
            pltpu.VMEM((n_head, 2 * rows, 2 * head_size), bf16),
            pltpu.VMEM((n_src, 2 * rows, 2 * head_size), bf16),
            pltpu.VMEM((q_dev * q_rows, head_size), f32),
            pltpu.VMEM((head_size, q_dev * q_rows), bf16),
            pltpu.VMEM((1, q_dev * q_rows), f32),
            pltpu.VMEM((n_src * 2 * rows, 1), f32),
            pltpu.VMEM((2 * rows, head_size), f32),
            pltpu.VMEM((2 * rows, head_size), f32),
            pltpu.VMEM((1, q_dev * q_rows), f32),
            pltpu.VMEM((1, q_dev * q_rows), f32),
            pltpu.VMEM((head_size, q_dev * q_rows), f32),
            pltpu.SemaphoreType.DMA,
            pltpu.SemaphoreType.DMA,
            pltpu.SemaphoreType.DMA((6,)),
            pltpu.SemaphoreType.DMA((n_chunk - 1 + SLICES,)),
            pltpu.SemaphoreType.DMA((n_chunk - 1 + SLICES,)),
            pltpu.SemaphoreType.DMA((n_chunk + 1, n_peer)),
            pltpu.SemaphoreType.DMA((n_chunk + 1, n_peer + 1)),
            pltpu.SemaphoreType.REGULAR,
            pltpu.VMEM((CHUNKS[-2], width), bf16),
            pltpu.VMEM((CHUNKS[-2], width), bf16),
            pltpu.VMEM((n_head, CHUNKS[-2], 2 * head_size), bf16),
            pltpu.VMEM((CHUNKS[-2], head_size), f32),
            pltpu.VMEM((CHUNKS[-2], head_size), f32),
            pltpu.SemaphoreType.DMA((4,)),
            pltpu.SemaphoreType.DMA((n_peer,)),
        ],
        compiler_params=pltpu.CompilerParams(
            collective_id=0, has_side_effects=True, vmem_limit_bytes=VMEM_LIMIT
        ),
    )(
        *[
            pltpu.with_memory_space_constraint(array, pltpu.HBM)
            for array in (
                hidden.reshape(rows, width),
                block_owner.reshape(1, -1),
                norm_gain[None],
                kv_weight,
                key_gain[None],
                queries,
                query_pos[None],
                freq,
            )
        ]
    )


def solution(mesh):
    in_specs = (
        P(("groups", "ctx", "hst", "head"), None, None),
        P("groups", None),
        P(),
        P(None, "hst"),
        P(),
        P(("groups", "ctx"), ("hst", "head")),
        P(("groups", "ctx")),
    )
    out_specs = P(("groups", "ctx"), ("hst", "head"))
    return jax.shard_map(body, mesh=mesh, in_specs=in_specs, out_specs=out_specs, check_vma=False)
```
